32 devices in a mesh: fsdp: 8 (over z, core), tp: 4 (over y, x).
Axes of the slice: x: 2, y: 2, z: 4, core: 2. Of those that a mesh axis runs over, the one named last changes fastest.
Arguments:
- tokens: float32 [3, 1024, 2048], P(None, 'fsdp'), may hold values from -6 to 6
- cotangent: float32 [3, 1024, 2048], P(None, 'fsdp'), may hold values from -6 to 6
- w_query: bfloat16 [2048, 2048], P('fsdp', 'tp'), may hold values from -0.125 to 0.125
- w_key: bfloat16 [2048, 2048], P('fsdp', 'tp'), may hold values from -0.125 to 0.125
- w_value: bfloat16 [2048, 2048], P('fsdp', 'tp'), may hold values from -0.125 to 0.125
- w_out: bfloat16 [2048, 2048], P('tp', 'fsdp'), may hold values from -0.125 to 0.125
- query_gain: bfloat16 [2048], P(('tp', 'fsdp')), may hold values from 0.25 to 1.75
- key_gain: bfloat16 [2048], P(('tp', 'fsdp')), may hold values from 0.25 to 1.75
- attn_gain: bfloat16 [2048], P('fsdp'), may hold values from 0.25 to 1.75
- w_gate: bfloat16 [2048, 8192], P('fsdp', 'tp'), may hold values from -0.125 to 0.125
- w_up: bfloat16 [2048, 8192], P('fsdp', 'tp'), may hold values from -0.125 to 0.125
- w_down: bfloat16 [8192, 2048], P('tp', 'fsdp'), may hold values from -0.0625 to 0.0625
- mlp_gain: bfloat16 [2048], P('fsdp'), may hold values from 0.25 to 1.75
- group_ids: int32 [3, 1], replicated, may hold values from 0 to 1
- span_order: int32 [16], replicated, may hold values from 0 to 15, each once
Outputs:
- layer_out: float32 [3, 1024, 2048], P(None, 'fsdp')
- input_grad: float32 [3, 1024, 2048], P(None, 'fsdp')
- grad_query: float32 [2048, 2048], P('fsdp', 'tp')
- grad_key: float32 [2048, 2048], P('fsdp', 'tp')
- grad_value: float32 [2048, 2048], P('fsdp', 'tp')
- grad_out: float32 [2048, 2048], P('tp', 'fsdp')
- grad_query_gain: float32 [2048], P(('tp', 'fsdp'))
- grad_key_gain: float32 [2048], P(('tp', 'fsdp'))
- grad_attn_gain: float32 [2048], P('fsdp')
- grad_gate: float32 [2048, 8192], P('fsdp', 'tp')
- grad_up: float32 [2048, 8192], P('fsdp', 'tp')
- grad_down: float32 [8192, 2048], P('tp', 'fsdp')
- grad_mlp_gain: float32 [2048], P('fsdp')
- grad_out_groups: float32 [2, 2048, 2048], P(None, 'tp', 'fsdp')
The draws below stay inside these ranges and needn't reach their ends.
Inputs may be any that keep to these rules, and one draw needn't show every extreme that they name: `span_order`: a permutation: every stored span holds a different block of 64 positions. `group_ids`: every group holds at least one sequence.
All inputs are finite; a program needn't handle non-finite values.
Results may differ from the reference program's by a relative error of at most 0.024.
Values may be sent and summed in bfloat16 or wider, within the bound.
No kernel may reach another device: no remote copies, remote signals or barrier semaphores. Data moves between devices by JAX's collectives and lax.ppermute only.
A program may use at most 192 MiB of HBM per device.

```python
import jax
import jax.numpy as jnp
from jax import lax

D = 2048
HEAD_DIM = 128
FF = 8192
TOK_SPAN = 64
ROWS = 3
GROUPS = 2
SPANS = 16
SEQ = 1024


def shard_levels(stream_key, shape, shards, low, top_value):
    level = 1.0
    for dim, parts in shards:
        steps = jax.random.uniform(jax.random.fold_in(jax.random.fold_in(stream_key, 6), dim), (parts,), jnp.float32, low / len(shards), top_value / len(shards))
        level = level * jnp.repeat(jnp.exp(steps), shape[dim] // parts).reshape((-1,) + (1,) * (len(shape) - 1 - dim))
    return level


def choose_distinct(stream_key, rows, amount, top, lift):
    sequence = jax.random.permutation(jax.random.fold_in(stream_key, 1), amount)
    boost = sequence
    for power in range(3):
        boost = boost * boost // amount
    boost = boost * lift // amount
    tickets = jax.random.randint(jax.random.fold_in(stream_key, 2), (rows, amount), 0, 4096) + boost
    fixed_rows = jax.random.permutation(jax.random.fold_in(stream_key, 3), rows)[jnp.arange(amount) % rows]
    tickets = jnp.where(jnp.arange(rows)[:, None] == fixed_rows[None, :], 1 << 14, tickets)
    merit = tickets * amount + jnp.arange(amount)
    return lax.top_k(merit.astype(jnp.int32), top)[1].astype(jnp.int32)


def centred(rng, dims, scale, bound, shards=(), kind=jnp.bfloat16):
    drawn = jax.random.normal(rng, dims, jnp.float32) * scale
    if len(shards) > 0:
        drawn = shard_levels(rng, dims, shards, -0.22, 0.18) * drawn
    return jnp.clip(drawn, min=-bound, max=bound).astype(kind)


def setup_inputs(seed: int = 0) -> dict:
    arg_keys = jax.random.split(jax.random.key(seed), 16)
    tokens = centred(arg_keys[0], (ROWS, SEQ, D), 1.0, 6.0, ((1, 8),), jnp.float32)
    cotangent = centred(arg_keys[1], (ROWS, SEQ, D), 1.0, 6.0, ((1, 8),), jnp.float32)
    w_query = centred(arg_keys[2], (D, D), D ** -0.5, 0.125, ((0, 8), (1, 4)))
    w_key = centred(arg_keys[3], (D, D), D ** -0.5, 0.125, ((0, 8), (1, 4)))
    w_value = centred(arg_keys[4], (D, D), D ** -0.5, 0.125, ((0, 8), (1, 4)))
    w_out = centred(arg_keys[5], (D, D), D ** -0.5, 0.125, ((0, 4), (1, 8)))
    query_gain = jnp.clip(1.0 + 0.15 * jax.random.normal(arg_keys[6], (D,), jnp.float32), 0.25, 1.75).astype(jnp.bfloat16)
    key_gain = jnp.clip(1.0 + 0.15 * jax.random.normal(arg_keys[7], (D,), jnp.float32), 0.25, 1.75).astype(jnp.bfloat16)
    attn_gain = jnp.clip(1.0 + 0.15 * jax.random.normal(arg_keys[8], (D,), jnp.float32), 0.25, 1.75).astype(jnp.bfloat16)
    w_gate = centred(arg_keys[9], (D, FF), D ** -0.5, 0.125, ((0, 8), (1, 4)))
    w_up = centred(arg_keys[10], (D, FF), D ** -0.5, 0.125, ((0, 8), (1, 4)))
    w_down = centred(arg_keys[11], (FF, D), FF ** -0.5, 0.0625, ((0, 4), (1, 8)))
    mlp_gain = jnp.clip(1.0 + 0.15 * jax.random.normal(arg_keys[12], (D,), jnp.float32), 0.25, 1.75).astype(jnp.bfloat16)
    group_ids = choose_distinct(arg_keys[13], ROWS, GROUPS, 1, 0)
    span_order = jax.random.permutation(arg_keys[14], SPANS).astype(jnp.int32)
    return {"tokens": tokens, "cotangent": cotangent, "w_query": w_query, "w_key": w_key, "w_value": w_value, "w_out": w_out, "query_gain": query_gain, "key_gain": key_gain, "attn_gain": attn_gain, "w_gate": w_gate, "w_up": w_up, "w_down": w_down, "mlp_gain": mlp_gain, "group_ids": group_ids, "span_order": span_order}


epsilon = 1e-06
rope_base = 500000.0
highest = lax.Precision.HIGHEST

@jax.custom_vjp
def low(v):
    return lax.optimization_barrier(v.astype(jnp.bfloat16)).astype(jnp.float32)

@jax.custom_vjp
def low_back(v):
    return v

def low_keep(v):
    return (low(v), None)

def low_pass(kept, grad):
    return (grad,)

def back_keep(v):
    return (v, None)

def back_low(kept, grad):
    return (low(grad),)
low.defvjp(low_keep, low_pass)
low_back.defvjp(back_keep, back_low)

def normed(inputs, gain):
    return inputs * lax.rsqrt(lax.optimization_barrier(jnp.mean(inputs * inputs, axis=-1, keepdims=True)) + epsilon) * gain

def rotary(inputs, positions):
    half_dim = HEAD_DIM // 2
    inv_freq = jnp.power(rope_base, -(jnp.arange(half_dim, dtype=jnp.float32) * 2.0 / HEAD_DIM))
    angles = positions.astype(jnp.float32)[:, None] * inv_freq[None, :]
    cosine = jnp.cos(angles)[None, :, None, :]
    sine = jnp.sin(angles)[None, :, None, :]
    front_half = inputs[..., :half_dim]
    back_half = inputs[..., half_dim:]
    return jnp.concatenate([front_half * cosine - back_half * sine, back_half * cosine + front_half * sine], axis=-1)

def project_full(inputs, matrix):
    return jnp.einsum('rsd,de->rse', inputs, matrix, precision=highest)

def one_head(operands, visible):
    query_h, key_h, value_h = operands
    scores = low_back(jnp.einsum('rqd,rkd->rqk', query_h, key_h, precision=highest) * HEAD_DIM ** (-0.5))
    scores = jnp.where(visible[None], scores, -1e+30)
    attn_prob = low(jax.nn.softmax(scores, axis=-1))
    return jnp.einsum('rqk,rkd->rqd', attn_prob, value_h, precision=highest)

def forward(tokens_in, weights, positions, group_ids):
    query_w, key_w, value_w, out_w, query_g, key_g, attn_g, gate_w, up_w, down_w, mlp_g, group_extra = weights
    batch_rows, seq_len, model_width = tokens_in.shape
    head_count = model_width // HEAD_DIM
    head_shape = (batch_rows, seq_len, head_count, HEAD_DIM)
    tokens_low = low(tokens_in)
    queries = low_back(project_full(tokens_low, query_w))
    keys = low_back(project_full(tokens_low, key_w))
    values = low(low_back(project_full(tokens_low, value_w))).reshape(head_shape)
    query_rot = low(rotary(normed(queries, query_g).reshape(head_shape), positions))
    key_rot = low(rotary(normed(keys, key_g).reshape(head_shape), positions))
    visible = positions[None, :] <= positions[:, None]

    def head_major(inputs):
        return jnp.transpose(inputs, (2, 0, 1, 3))
    heads_out = lax.map(jax.checkpoint(lambda operands: one_head(operands, visible)), (head_major(query_rot), head_major(key_rot), head_major(values)))
    attended = low(low_back(jnp.transpose(heads_out, (1, 2, 0, 3)).reshape(batch_rows, seq_len, model_width)))
    out_rows = out_w[None] + group_extra[group_ids[:, 0]]
    branch_attn = low_back(jnp.einsum('rsd,rde->rse', attended, out_rows, precision=highest))
    hidden = tokens_in + normed(branch_attn, attn_g)
    hidden_low = low(hidden)
    gate_act = low_back(project_full(hidden_low, gate_w))
    up_act = low_back(project_full(hidden_low, up_w))
    mixed = low(jax.nn.silu(gate_act) * up_act)
    branch_mlp = low_back(project_full(mixed, down_w))
    return hidden + normed(branch_mlp, mlp_g)

def reference(tokens, cotangent, w_query, w_key, w_value, w_out, query_gain, key_gain, attn_gain, w_gate, w_up, w_down, mlp_gain, group_ids, span_order):
    storage = jnp.arange(SEQ, dtype=jnp.int32)
    positions = (span_order[storage // TOK_SPAN] * TOK_SPAN + storage % TOK_SPAN).astype(jnp.int32)
    params = tuple((weight.astype(jnp.float32) for weight in (w_query, w_key, w_value, w_out, query_gain, key_gain, attn_gain, w_gate, w_up, w_down, mlp_gain)))
    group_extra = jnp.zeros((GROUPS, D, D), jnp.float32)

    def layer(tokens_in, *weights):
        return forward(tokens_in, weights, positions, group_ids)
    layer_out, pullback = jax.vjp(layer, tokens, *params, group_extra)
    grads = pullback(cotangent)
    return (layer_out, grads[0], grads[1], grads[2], grads[3], grads[4], grads[5], grads[6], grads[7], grads[8], grads[9], grads[10], grads[11], grads[12])
```

```python
from functools import partial

import jax
import jax.numpy as jnp
from jax import lax
from jax.experimental import pallas as pl
from jax.sharding import PartitionSpec as P

HEAD_DIM = 128
GROUPS = 2


epsilon = 1e-06
rope_base = 500000.0


def positions_of(span_order, start_row, count, span_len):
    row_index = start_row + jnp.arange(count, dtype=jnp.int32)
    span_ids = row_index // span_len
    span_table = jnp.arange(span_order.shape[0], dtype=jnp.int32)
    picked = jnp.sum(
        jnp.where(span_ids[:, None] == span_table[None, :], span_order[None, :], 0), axis=1
    )
    return picked * span_len + row_index % span_len


def rotary(inputs, positions, direction):
    half_dim = inputs.shape[-1] // 2
    inv_freq = jnp.power(
        rope_base, -(jnp.arange(half_dim, dtype=jnp.float32) * 2.0 / inputs.shape[-1])
    )
    angles = positions.astype(jnp.float32)[:, None] * inv_freq[None, :]
    cosine = jnp.cos(angles)[None, :, None, :]
    sine = direction * jnp.sin(angles)[None, :, None, :]
    front_half = inputs[..., :half_dim]
    back_half = inputs[..., half_dim:]
    return jnp.concatenate(
        [front_half * cosine - back_half * sine, back_half * cosine + front_half * sine], axis=-1
    )


def score_block(query_rot, key_rot, query_pos, key_pos):
    raw_scores = jnp.einsum(
        "rqhd,rkhd->rhqk", query_rot, key_rot, preferred_element_type=jnp.float32
    )
    scaled = raw_scores * query_rot.shape[-1] ** (-0.5)
    visible = key_pos[None, :] <= query_pos[:, None]
    return (scaled, visible)


def attend(query_rot, keys_all, values_all, query_pos, key_pos):
    scaled, visible = score_block(query_rot, keys_all, query_pos, key_pos)
    scaled = jnp.where(visible[None, None], scaled, -1e30)
    row_peak = jnp.max(scaled, axis=-1, keepdims=True)
    log_total = row_peak + jnp.log(jnp.sum(jnp.exp(scaled - row_peak), axis=-1, keepdims=True))
    attn_prob = jnp.exp(scaled - log_total).astype(jnp.bfloat16)
    attended = jnp.einsum(
        "rhqk,rkhd->rqhd", attn_prob, values_all, preferred_element_type=jnp.float32
    )
    return (attended, log_total[..., 0])


def query_step(
    carried,
    pieces,
    start_row,
    query_rot,
    grad_attended,
    log_total,
    row_delta,
    query_pos,
    span_order,
    span_len,
    skipping,
):
    key_piece, value_piece = pieces
    key_pos = positions_of(span_order, start_row, key_piece.shape[1], span_len)
    scaled, visible = score_block(query_rot, key_piece, query_pos, key_pos)
    attn_prob = jnp.where(visible[None, None], jnp.exp(scaled - log_total[..., None]), 0.0)
    grad_prob = jnp.einsum(
        "rqhd,rkhd->rhqk", grad_attended, value_piece, preferred_element_type=jnp.float32
    )
    grad_scores = (attn_prob * (grad_prob - row_delta[..., None])).astype(jnp.bfloat16)
    return jnp.einsum("rhqk,rkhd->rqhd", grad_scores, key_piece, preferred_element_type=jnp.float32)


def key_step(
    carried,
    pieces,
    start_row,
    key_rot,
    values_low,
    key_pos,
    lse_all,
    delta_all,
    span_order,
    span_len,
    skipping,
):
    query_low, grad_low = pieces
    count = query_low.shape[1]
    query_pos = positions_of(span_order, start_row, count, span_len)
    scaled, visible = score_block(query_low, key_rot, query_pos, key_pos)
    lse_rows = jnp.transpose(lse_all, (0, 2, 1))[..., None]
    delta_rows = jnp.transpose(delta_all, (0, 2, 1))[..., None]
    attn_prob = jnp.where(visible[None, None], jnp.exp(scaled - lse_rows), 0.0)
    grad_values = jnp.einsum(
        "rhqk,rqhd->rkhd",
        attn_prob.astype(jnp.bfloat16),
        grad_low,
        preferred_element_type=jnp.float32,
    )
    grad_prob = jnp.einsum(
        "rqhd,rkhd->rhqk", grad_low, values_low, preferred_element_type=jnp.float32
    )
    grad_scores = (attn_prob * (grad_prob - delta_rows)).astype(jnp.bfloat16)
    grad_keys = jnp.einsum(
        "rhqk,rqhd->rkhd", grad_scores, query_low, preferred_element_type=jnp.float32
    )
    return (grad_keys, grad_values)


def norm_back(branch, inv_root, gain, grad_output):
    gained = grad_output * gain
    grad_gain = jnp.sum(grad_output * branch * inv_root, axis=(0, 1))
    row_total = jnp.sum(branch * gained, axis=-1, keepdims=True)
    grad_branch = inv_root * gained - branch * inv_root**3 * row_total / branch.shape[-1]
    return (grad_gain, grad_branch)


def local(
    tokens,
    cotangent,
    w_query,
    w_key,
    w_value,
    w_out,
    query_gain,
    key_gain,
    attn_gain,
    w_gate,
    w_up,
    w_down,
    mlp_gain,
    group_ids,
    span_order,
):
    batch_rows, local_len, model_width = tokens.shape
    span_len = local_len // 2
    seq_len = local_len * lax.axis_size("fsdp")
    query_pos = positions_of(span_order, lax.axis_index("fsdp") * local_len, local_len, span_len)
    all_pos = positions_of(span_order, 0, seq_len, span_len)
    attn_set = (
        lax.all_gather(w_query, "fsdp", axis=0, tiled=True),
        lax.all_gather(w_key, "fsdp", axis=0, tiled=True),
        lax.all_gather(w_value, "fsdp", axis=0, tiled=True),
        lax.all_gather(w_out, "fsdp", axis=1, tiled=True),
        lax.all_gather(query_gain, "fsdp", axis=0, tiled=True),
        lax.all_gather(key_gain, "fsdp", axis=0, tiled=True),
        lax.all_gather(attn_gain, "fsdp", axis=0, tiled=True),
    )
    gain_query = attn_set[4].astype(jnp.float32)
    gain_key = attn_set[5].astype(jnp.float32)
    gain_attn = attn_set[6].astype(jnp.float32)
    tokens_low = tokens.astype(jnp.bfloat16)
    queries = jnp.einsum("rsd,de->rse", tokens_low, attn_set[0], preferred_element_type=jnp.float32)
    keys = jnp.einsum("rsd,de->rse", tokens_low, attn_set[1], preferred_element_type=jnp.float32)
    values = jnp.einsum("rsd,de->rse", tokens_low, attn_set[2], preferred_element_type=jnp.float32)
    square_sums = lax.psum(
        (jnp.sum(queries * queries, axis=-1), jnp.sum(keys * keys, axis=-1)), "tp"
    )
    query_scale = lax.rsqrt(square_sums[0] / model_width + epsilon)[..., None]
    key_scale = lax.rsqrt(square_sums[1] / model_width + epsilon)[..., None]
    local_width = queries.shape[-1]
    head_count = local_width // HEAD_DIM
    head_shape = (batch_rows, local_len, head_count, HEAD_DIM)
    query_rot = rotary(
        (queries * query_scale * gain_query).reshape(head_shape), query_pos, 1.0
    ).astype(jnp.bfloat16)
    key_rot = rotary((keys * key_scale * gain_key).reshape(head_shape), query_pos, 1.0).astype(
        jnp.bfloat16
    )
    values_low = values.astype(jnp.bfloat16).reshape(head_shape)
    keys_gathered, values_gathered = (
        lax.all_gather(key_rot, "fsdp", axis=1, tiled=True),
        lax.all_gather(values_low, "fsdp", axis=1, tiled=True),
    )
    attended, log_total = attend(query_rot, keys_gathered, values_gathered, query_pos, all_pos)
    attended_low = attended.reshape(batch_rows, local_len, local_width).astype(jnp.bfloat16)
    branch_attn = lax.psum(
        jnp.einsum(
            "rse,ed->rsd", attended_low, attn_set[3], preferred_element_type=jnp.float32
        ).astype(jnp.bfloat16),
        "tp",
    ).astype(jnp.float32)
    attn_norm = lax.rsqrt(jnp.mean(branch_attn * branch_attn, axis=-1, keepdims=True) + epsilon)
    hidden = tokens + branch_attn * attn_norm * gain_attn
    mlp_set = (
        lax.all_gather(w_gate, "fsdp", axis=0, tiled=True),
        lax.all_gather(w_up, "fsdp", axis=0, tiled=True),
        lax.all_gather(w_down, "fsdp", axis=1, tiled=True),
        lax.all_gather(mlp_gain, "fsdp", axis=0, tiled=True),
    )
    gain_mlp = mlp_set[3].astype(jnp.float32)
    hidden_low = hidden.astype(jnp.bfloat16)
    gate_act = jnp.einsum("rsd,df->rsf", hidden_low, mlp_set[0], preferred_element_type=jnp.float32)
    up_act = jnp.einsum("rsd,df->rsf", hidden_low, mlp_set[1], preferred_element_type=jnp.float32)
    mixed_low = (jax.nn.silu(gate_act) * up_act).astype(jnp.bfloat16)
    branch_mlp = lax.psum(
        jnp.einsum("rsf,fd->rsd", mixed_low, mlp_set[2], preferred_element_type=jnp.float32).astype(
            jnp.bfloat16
        ),
        "tp",
    ).astype(jnp.float32)
    mlp_norm = lax.rsqrt(jnp.mean(branch_mlp * branch_mlp, axis=-1, keepdims=True) + epsilon)
    layer_out = hidden + branch_mlp * mlp_norm * gain_mlp
    back_set = (
        lax.all_gather(w_query, "fsdp", axis=0, tiled=True),
        lax.all_gather(w_key, "fsdp", axis=0, tiled=True),
        lax.all_gather(w_value, "fsdp", axis=0, tiled=True),
        lax.all_gather(w_out, "fsdp", axis=1, tiled=True),
        lax.all_gather(w_gate, "fsdp", axis=0, tiled=True),
        lax.all_gather(w_up, "fsdp", axis=0, tiled=True),
        lax.all_gather(w_down, "fsdp", axis=1, tiled=True),
    )
    query_back, key_back, value_back, out_back, gate_back, up_back, down_back = back_set
    grad_gain_mlp, grad_branch_mlp = norm_back(branch_mlp, mlp_norm, gain_mlp, cotangent)
    grad_mlp_low = grad_branch_mlp.astype(jnp.bfloat16)
    grad_down_w = jnp.einsum(
        "rsf,rsd->fd", mixed_low, grad_mlp_low, preferred_element_type=jnp.float32
    )
    grad_mixed = jnp.einsum(
        "rsd,fd->rsf", grad_mlp_low, down_back, preferred_element_type=jnp.float32
    )
    gate_sigma = jax.nn.sigmoid(gate_act)
    grad_gate_act = (
        grad_mixed * up_act * gate_sigma * (1.0 + gate_act * (1.0 - gate_sigma))
    ).astype(jnp.bfloat16)
    grad_up_act = (grad_mixed * gate_act * gate_sigma).astype(jnp.bfloat16)
    mlp_back_in = jnp.einsum(
        "rsf,df->rsd", grad_gate_act, gate_back, preferred_element_type=jnp.float32
    ) + jnp.einsum("rsf,df->rsd", grad_up_act, up_back, preferred_element_type=jnp.float32)
    grad_hidden = cotangent + lax.psum(mlp_back_in.astype(jnp.bfloat16), "tp").astype(jnp.float32)
    grad_gate_w = jnp.einsum(
        "rsd,rsf->df", hidden_low, grad_gate_act, preferred_element_type=jnp.float32
    )
    grad_up_w = jnp.einsum(
        "rsd,rsf->df", hidden_low, grad_up_act, preferred_element_type=jnp.float32
    )
    grad_gain_attn, grad_branch_attn = norm_back(branch_attn, attn_norm, gain_attn, grad_hidden)
    grad_attn_low = grad_branch_attn.astype(jnp.bfloat16)
    per_row = jnp.einsum(
        "rse,rsd->red", attended_low, grad_attn_low, preferred_element_type=jnp.float32
    )
    member = (group_ids[:, 0][:, None] == jnp.arange(GROUPS, dtype=jnp.int32)[None, :]).astype(
        jnp.float32
    )
    grad_out_groups = jnp.sum(member[:, :, None, None] * per_row[:, None], axis=0)
    grad_out_w = jnp.sum(per_row, axis=0)
    grad_attended_low = (
        jnp.einsum("rsd,ed->rse", grad_attn_low, out_back, preferred_element_type=jnp.float32)
        .reshape(head_shape)
        .astype(jnp.bfloat16)
    )
    delta_rows = jnp.sum(grad_attended_low.astype(jnp.float32) * attended, axis=-1)
    row_delta = jnp.transpose(delta_rows, (0, 2, 1))
    zero_grad = jnp.zeros(head_shape, jnp.float32)
    query_fn = partial(
        query_step,
        query_rot=query_rot,
        grad_attended=grad_attended_low,
        log_total=log_total,
        row_delta=row_delta,
        query_pos=query_pos,
        span_order=span_order,
        span_len=span_len,
        skipping=False,
    )
    grad_query_rot = query_fn(
        zero_grad,
        (
            lax.all_gather(key_rot, "fsdp", axis=1, tiled=True),
            lax.all_gather(values_low, "fsdp", axis=1, tiled=True),
        ),
        jnp.int32(0),
    )
    lse_rows = jnp.transpose(log_total, (0, 2, 1))
    lse_all, delta_all = (
        lax.all_gather(lse_rows, "fsdp", axis=1, tiled=True),
        lax.all_gather(delta_rows, "fsdp", axis=1, tiled=True),
    )
    key_fn = partial(
        key_step,
        key_rot=key_rot,
        values_low=values_low,
        key_pos=query_pos,
        lse_all=lse_all,
        delta_all=delta_all,
        span_order=span_order,
        span_len=span_len,
        skipping=False,
    )
    grad_key_rot, grad_values = key_fn(
        (zero_grad, zero_grad),
        (
            lax.all_gather(query_rot, "fsdp", axis=1, tiled=True),
            lax.all_gather(grad_attended_low, "fsdp", axis=1, tiled=True),
        ),
        jnp.int32(0),
    )
    scaling = HEAD_DIM ** (-0.5)
    grad_qn = rotary(grad_query_rot * scaling, query_pos, -1.0).reshape(
        batch_rows, local_len, local_width
    )
    grad_kn = rotary(grad_key_rot * scaling, query_pos, -1.0).reshape(
        batch_rows, local_len, local_width
    )
    gained_query = grad_qn * gain_query
    gained_key = grad_kn * gain_key
    cross_sums = lax.psum(
        (jnp.sum(queries * gained_query, axis=-1), jnp.sum(keys * gained_key, axis=-1)), "tp"
    )
    grad_gain_query = jnp.sum(grad_qn * queries * query_scale, axis=(0, 1))
    grad_gain_key = jnp.sum(grad_kn * keys * key_scale, axis=(0, 1))
    grad_queries = (
        query_scale * gained_query
        - queries * query_scale**3 * cross_sums[0][..., None] / model_width
    ).astype(jnp.bfloat16)
    grad_keys = (
        key_scale * gained_key - keys * key_scale**3 * cross_sums[1][..., None] / model_width
    ).astype(jnp.bfloat16)
    grad_values_low = grad_values.reshape(batch_rows, local_len, local_width).astype(jnp.bfloat16)
    attn_back_in = jnp.einsum(
        "rse,de->rsd", grad_queries, query_back, preferred_element_type=jnp.float32
    )
    attn_back_in = attn_back_in + jnp.einsum(
        "rse,de->rsd", grad_keys, key_back, preferred_element_type=jnp.float32
    )
    attn_back_in = attn_back_in + jnp.einsum(
        "rse,de->rsd", grad_values_low, value_back, preferred_element_type=jnp.float32
    )
    input_grad = grad_hidden + lax.psum(attn_back_in.astype(jnp.bfloat16), "tp").astype(jnp.float32)
    grad_query_w = jnp.einsum(
        "rsd,rse->de", tokens_low, grad_queries, preferred_element_type=jnp.float32
    )
    grad_key_w = jnp.einsum(
        "rsd,rse->de", tokens_low, grad_keys, preferred_element_type=jnp.float32
    )
    grad_value_w = jnp.einsum(
        "rsd,rse->de", tokens_low, grad_values_low, preferred_element_type=jnp.float32
    )
    summed = (
        lax.psum_scatter(
            grad_query_w.astype(jnp.bfloat16), "fsdp", scatter_dimension=0, tiled=True
        ).astype(jnp.float32),
        lax.psum_scatter(
            grad_key_w.astype(jnp.bfloat16), "fsdp", scatter_dimension=0, tiled=True
        ).astype(jnp.float32),
        lax.psum_scatter(
            grad_value_w.astype(jnp.bfloat16), "fsdp", scatter_dimension=0, tiled=True
        ).astype(jnp.float32),
        lax.psum_scatter(
            grad_out_w.astype(jnp.bfloat16), "fsdp", scatter_dimension=1, tiled=True
        ).astype(jnp.float32),
        lax.psum_scatter(
            grad_out_groups.astype(jnp.bfloat16), "fsdp", scatter_dimension=2, tiled=True
        ).astype(jnp.float32),
        lax.psum_scatter(
            grad_gain_query.astype(jnp.bfloat16), "fsdp", scatter_dimension=0, tiled=True
        ).astype(jnp.float32),
        lax.psum_scatter(
            grad_gain_key.astype(jnp.bfloat16), "fsdp", scatter_dimension=0, tiled=True
        ).astype(jnp.float32),
        lax.psum_scatter(
            grad_gain_attn.astype(jnp.bfloat16), "fsdp", scatter_dimension=0, tiled=True
        ).astype(jnp.float32),
        lax.psum_scatter(
            grad_gate_w.astype(jnp.bfloat16), "fsdp", scatter_dimension=0, tiled=True
        ).astype(jnp.float32),
        lax.psum_scatter(
            grad_up_w.astype(jnp.bfloat16), "fsdp", scatter_dimension=0, tiled=True
        ).astype(jnp.float32),
        lax.psum_scatter(
            grad_down_w.astype(jnp.bfloat16), "fsdp", scatter_dimension=1, tiled=True
        ).astype(jnp.float32),
        lax.psum_scatter(
            grad_gain_mlp.astype(jnp.bfloat16), "fsdp", scatter_dimension=0, tiled=True
        ).astype(jnp.float32),
    )
    return (
        layer_out,
        input_grad,
        summed[0],
        summed[1],
        summed[2],
        summed[3],
        summed[5],
        summed[6],
        summed[7],
        summed[8],
        summed[9],
        summed[10],
        summed[11],
        summed[4],
    )


def attend_kernel(q_ref, kv_ref, qpos_ref, kpos_ref, ks_ref, out_ref, lse_ref):
    width = q_ref.shape[-1]
    head_of = (lax.broadcasted_iota(jnp.int32, (1, width), 1) // 64) % 2
    query = q_ref[0]
    qpos = qpos_ref[...]
    parts = kv_ref.shape[0]
    scaling = HEAD_DIM ** (-0.5)
    total = jnp.zeros(query.shape, jnp.float32)
    logs = []
    for head in range(2):
        picked = jnp.where(head_of == head, query, jnp.zeros_like(query))
        scores = []
        for part in range(parts):
            raw = lax.dot_general(
                picked,
                kv_ref[part, 0, :, :width],
                (((1,), (1,)), ((), ())),
                preferred_element_type=jnp.float32,
            )
            scaled = raw * (ks_ref[part, 0] * scaling)
            scores.append(jnp.where(kpos_ref[part] <= qpos, scaled, -1e30))
        peak = jnp.max(scores[0], axis=1, keepdims=True)
        for part in range(1, parts):
            peak = jnp.maximum(peak, jnp.max(scores[part], axis=1, keepdims=True))
        sums = jnp.zeros_like(peak)
        for part in range(parts):
            scores[part] = jnp.exp(scores[part] - peak)
            sums = sums + jnp.sum(scores[part], axis=1, keepdims=True)
        inverse = 1.0 / sums
        attended = jnp.zeros(query.shape, jnp.float32)
        for part in range(parts):
            attended = attended + jnp.dot(
                (scores[part] * inverse).astype(jnp.bfloat16),
                kv_ref[part, 0, :, width:],
                preferred_element_type=jnp.float32,
            )
        total = jnp.where(head_of == head, attended, total)
        logs.append(peak + jnp.log(sums))
    out_ref[0] = total
    lse_ref[0] = jnp.concatenate(logs, axis=1)


def attend_back_kernel(
    q_ref, kv_ref, grad_ref, out_ref, lse_ref, qpos_ref, kpos_ref, ks_ref, dq_ref, dkv_ref
):
    width = q_ref.shape[-1]
    head_of = (lax.broadcasted_iota(jnp.int32, (1, width), 1) // 64) % 2
    query = q_ref[0]
    grad = grad_ref[0]
    qpos = qpos_ref[...]
    parts = kv_ref.shape[0]
    scaling = HEAD_DIM ** (-0.5)
    product = grad.astype(jnp.float32) * out_ref[0]
    zero = jnp.zeros_like(query)
    queries = [jnp.where(head_of == head, query, zero) for head in range(2)]
    grads = [jnp.where(head_of == head, grad, zero) for head in range(2)]
    deltas = [
        jnp.sum(jnp.where(head_of == head, product, 0.0), axis=1, keepdims=True)
        for head in range(2)
    ]
    totals = [jnp.zeros(query.shape, jnp.float32) for _ in range(2)]
    for part in range(parts):
        key = kv_ref[part, 0, :, :width]
        value = kv_ref[part, 0, :, width:]
        visible = kpos_ref[part] <= qpos
        key_scale = ks_ref[part, 0]
        grad_key = []
        grad_value = []
        for head in range(2):
            raw = lax.dot_general(
                queries[head], key, (((1,), (1,)), ((), ())), preferred_element_type=jnp.float32
            )
            scaled = raw * (key_scale * scaling)
            prob = jnp.where(visible, jnp.exp(scaled - lse_ref[0, :, head : head + 1]), 0.0)
            grad_value.append(
                lax.dot_general(
                    prob.astype(jnp.bfloat16),
                    grad,
                    (((0,), (0,)), ((), ())),
                    preferred_element_type=jnp.float32,
                )
            )
            grad_prob = lax.dot_general(
                grads[head], value, (((1,), (1,)), ((), ())), preferred_element_type=jnp.float32
            )
            grad_scores = (prob * (grad_prob - deltas[head]) * key_scale).astype(jnp.bfloat16)
            totals[head] = totals[head] + jnp.dot(
                grad_scores, key, preferred_element_type=jnp.float32
            )
            grad_key.append(
                lax.dot_general(
                    grad_scores,
                    query,
                    (((0,), (0,)), ((), ())),
                    preferred_element_type=jnp.float32,
                )
            )
        dkv_ref[part, 0, :, :width] = (
            jnp.where(head_of == 0, grad_key[0], grad_key[1]) * scaling
        ).astype(jnp.bfloat16)
        dkv_ref[part, 0, :, width:] = jnp.where(head_of == 0, grad_value[0], grad_value[1]).astype(
            jnp.bfloat16
        )
    dq_ref[0] = jnp.where(head_of == 0, totals[0], totals[1]) * scaling


def attention_specs(rows, parts, count, width):
    row = pl.BlockSpec((1, count, width), lambda r: (r, 0, 0))
    both = pl.BlockSpec((parts, 1, count, 2 * width), lambda r: (0, r, 0, 0))
    qpos = pl.BlockSpec((count, 1), lambda r: (0, 0))
    kpos = pl.BlockSpec((parts, 1, count), lambda r: (0, 0, 0))
    scale = pl.BlockSpec((parts, 1, 1, count), lambda r: (0, r, 0, 0))
    logs = pl.BlockSpec((1, count, 2), lambda r: (r, 0, 0))
    return row, both, qpos, kpos, scale, logs


def attend_tiles(query, both, qpos, kpos, key_scale):
    rows, count, width = query.shape
    parts = both.shape[0]
    row, pair, qspec, kspec, scale, logs = attention_specs(rows, parts, count, width)
    return pl.pallas_call(
        attend_kernel,
        grid=(rows,),
        in_specs=[row, pair, qspec, kspec, scale],
        out_specs=[row, logs],
        out_shape=[
            jax.ShapeDtypeStruct((rows, count, width), jnp.float32),
            jax.ShapeDtypeStruct((rows, count, 2), jnp.float32),
        ],
        name="attend",
    )(query, both, qpos, kpos, key_scale)


def attend_back_tiles(query, both, grad, attended, log_total, qpos, kpos, key_scale):
    rows, count, width = query.shape
    parts = both.shape[0]
    row, pair, qspec, kspec, scale, logs = attention_specs(rows, parts, count, width)
    return pl.pallas_call(
        attend_back_kernel,
        grid=(rows,),
        in_specs=[row, pair, row, row, logs, qspec, kspec, scale],
        out_specs=[row, pair],
        out_shape=[
            jax.ShapeDtypeStruct((rows, count, width), jnp.float32),
            jax.ShapeDtypeStruct(both.shape, jnp.bfloat16),
        ],
        name="attend_back",
    )(query, both, grad, attended, log_total, qpos, kpos, key_scale)


def swap(value, axis, bit):
    size = lax.axis_size(axis)
    return lax.ppermute(value, axis, [(i, i ^ bit) for i in range(size)])


def spread(blocks, axis):
    return lax.all_to_all(blocks, axis, split_axis=0, concat_axis=0, tiled=True)


def share(value, axis):
    size = lax.axis_size(axis)
    return spread(jnp.broadcast_to(value[None], (size,) + value.shape), axis)


def gather_tp(piece, first):
    one = swap(piece, "tp", 1)
    two = swap(piece, "tp", 2)
    three = swap(one, "tp", 2) if first == 1 else swap(two, "tp", 1)
    return (piece, one, two, three)


def scatter_tp(keep, send, second, axis):
    first = 3 - second
    merged = keep + swap(send.astype(jnp.bfloat16), "tp", first).astype(jnp.float32)
    mine, other = jnp.split(merged, 2, axis=axis)
    return mine + swap(other.astype(jnp.bfloat16), "tp", second).astype(jnp.float32)


def arrival_rows(weight, chips):
    width = weight.shape[-1]
    view = weight.reshape(2, 2, chips, 2, 64, width).transpose(2, 0, 3, 1, 4, 5)
    return jnp.stack([view[:, 0], view[:, 1, ::-1]], axis=1).reshape(-1, width)


def natural_rows(grad, chips):
    width = grad.shape[-1]
    view = grad.reshape(chips, 2, 2, 2, 64, width)
    view = jnp.stack([view[:, 0], view[:, 1, ::-1]], axis=1)
    return view.transpose(1, 3, 0, 2, 4, 5).reshape(2 * 2, -1, width)


def matmul(lhs, rhs, dims):
    return lax.dot_general(lhs, rhs, (dims, ((), ())), preferred_element_type=jnp.float32)


def local_fast(
    tokens,
    cotangent,
    w_query,
    w_key,
    w_value,
    w_out,
    query_gain,
    key_gain,
    attn_gain,
    w_gate,
    w_up,
    w_down,
    mlp_gain,
    group_ids,
    span_order,
):
    low = jnp.bfloat16
    batch_rows, local_len, width = tokens.shape
    members = lax.axis_size("fsdp")
    parts = lax.axis_size("tp")
    chips = members // 2
    member = lax.axis_index("fsdp")
    part = lax.axis_index("tp")
    core = member % 2
    span_len = local_len // 2
    sub = local_len // parts
    count = members * sub
    tile = batch_rows * count
    pair = 2 * HEAD_DIM
    bundle = 4 * 64
    rows_local = w_query.shape[0]
    unit = w_gate.shape[1] // members

    own_tokens = lax.dynamic_slice_in_dim(tokens, part * sub, sub, axis=1)
    own_cotangent = lax.dynamic_slice_in_dim(cotangent, part * sub, sub, axis=1)

    def halves(weight):
        return weight.reshape(rows_local, members, 64)

    packed = jnp.concatenate(
        [halves(w_query), halves(w_key), halves(w_value), jnp.zeros_like(halves(w_value))], axis=2
    ).transpose(1, 0, 2)
    packed = spread(packed, "fsdp").reshape(width, bundle)
    gain_row = jnp.concatenate(
        [query_gain, key_gain, jnp.zeros((bundle - 2 * 64,), query_gain.dtype)]
    )
    packed = jnp.concatenate(
        [packed, jnp.broadcast_to(gain_row[None], (16, bundle)).astype(packed.dtype)], axis=0
    )
    token_low = lax.all_gather(own_tokens.astype(low), "fsdp", axis=1, tiled=True)
    packed = share(packed, "tp")
    own_half = lax.dynamic_slice_in_dim(packed, 2 * core, 2, axis=0)
    other_half = swap(lax.dynamic_slice_in_dim(packed, 2 - 2 * core, 2, axis=0), "fsdp", 1)

    norm_gains = jnp.concatenate(
        [attn_gain[None], mlp_gain[None], jnp.zeros((14, attn_gain.shape[0]), attn_gain.dtype)]
    )
    out_rows = lax.all_gather(
        jnp.concatenate([w_out, norm_gains.astype(w_out.dtype)], axis=0),
        "fsdp",
        axis=1,
        tiled=True,
    )
    gain_attn = out_rows[w_out.shape[0]].astype(jnp.float32)
    gain_mlp = out_rows[w_out.shape[0] + 1].astype(jnp.float32)
    out_full = lax.all_gather(out_rows[: w_out.shape[0]], "tp", axis=0, tiled=True)
    out_full = arrival_rows(out_full, chips)

    def columns(weight):
        return weight.reshape(rows_local, members, unit).transpose(1, 0, 2)

    gate_up = spread(jnp.stack([columns(w_gate), columns(w_up)], axis=1), "fsdp")
    down = spread(w_down.reshape(members, unit, rows_local), "fsdp")
    gate_all = jnp.concatenate(gather_tp(gate_up[:, 0].reshape(width, unit), 1), axis=1)
    up_all = jnp.concatenate(gather_tp(gate_up[:, 1].reshape(width, unit), 2), axis=1)
    down_all = jnp.concatenate(
        gather_tp(down.transpose(1, 0, 2).reshape(unit, width), 1), axis=0
    )

    index = jnp.arange(members, dtype=jnp.int32)[:, None] * local_len
    index = (index + jnp.arange(sub, dtype=jnp.int32)[None, :]).reshape(count)
    index = index[None, :] + jnp.arange(parts, dtype=jnp.int32)[:, None] * sub
    spans = jnp.arange(span_order.shape[0], dtype=jnp.int32)
    picked = jnp.sum(
        jnp.where((index // span_len)[..., None] == spans, span_order, 0), axis=-1
    )
    all_pos = picked * span_len + index % span_len
    query_pos = lax.dynamic_index_in_dim(all_pos, part, axis=0, keepdims=False)
    inv_freq = jnp.power(
        rope_base, -(jnp.arange(64, dtype=jnp.float32) * 2.0 / HEAD_DIM)
    )
    angles = query_pos.astype(jnp.float32)[:, None] * jnp.tile(inv_freq, 2)[None, :]
    cosine = jnp.cos(angles)[None]
    sine = (jnp.where(core == 0, 1.0, -1.0) * jnp.sin(angles))[None]

    def rotate(value, direction):
        own, other = value[..., :HEAD_DIM], value[..., HEAD_DIM:]
        turned = direction * sine
        return jnp.concatenate(
            [own * cosine - other * turned, other * cosine + own * turned], axis=-1
        )

    weight_pieces = [own_half[0], own_half[1], other_half[0], other_half[1]]
    acts = [
        matmul(token_low, piece[:width], ((2,), (0,))) for piece in weight_pieces
    ]

    def lanes(pieces, at):
        return jnp.concatenate([piece[..., at * 64 : at * 64 + 64] for piece in pieces], axis=-1)

    queries, keys, values = (lanes(acts, at) for at in range(3))
    gain_rows = [piece[width].astype(jnp.float32) for piece in weight_pieces]
    gain_query, gain_key = lanes(gain_rows, 0), lanes(gain_rows, 1)
    key_low = rotate(keys * gain_key, 1.0).astype(low)
    both = share(jnp.concatenate([key_low, values.astype(low)], axis=-1), "tp")
    square_sums = lax.psum(
        jnp.stack([jnp.sum(queries * queries, axis=-1), jnp.sum(keys * keys, axis=-1)]), "fsdp"
    )
    scales = lax.rsqrt(square_sums / width + epsilon)
    query_scale, key_scale = scales[0][..., None], scales[1][..., None]
    all_key_scale = share(scales[1], "tp").reshape(parts, batch_rows, 1, count)
    query_low = rotate(queries * query_scale * gain_query, 1.0).astype(low)
    qpos = query_pos[:, None]
    kpos = all_pos[:, None, :]
    attended, log_total = attend_tiles(query_low, both, qpos, kpos, all_key_scale)

    def to_tokens(value):
        blocks = value.reshape(batch_rows, members, sub, pair).transpose(1, 0, 2, 3)
        return spread(blocks, "fsdp").transpose(1, 2, 0, 3).reshape(batch_rows, sub, members * pair)

    def to_heads(value):
        blocks = value.reshape(batch_rows, sub, members, pair).transpose(2, 0, 1, 3)
        return spread(blocks, "fsdp").transpose(1, 0, 2, 3).reshape(batch_rows, count, pair)

    attended_low = attended.astype(low)
    branch_attn = matmul(to_tokens(attended_low), out_full, ((2,), (0,)))
    attn_norm = lax.rsqrt(jnp.mean(branch_attn * branch_attn, axis=-1, keepdims=True) + epsilon)
    hidden = own_tokens + branch_attn * attn_norm * gain_attn
    hidden_low = lax.all_gather(hidden.astype(low), "fsdp", axis=1, tiled=True)

    gate_act = matmul(hidden_low, gate_all, ((2,), (0,)))
    up_act = matmul(hidden_low, up_all, ((2,), (0,)))
    gate_sigma = jax.nn.sigmoid(gate_act)
    mixed_low = (gate_act * gate_sigma * up_act).astype(low)
    branch_mlp = lax.psum_scatter(
        matmul(mixed_low, down_all, ((2,), (0,))).astype(low),
        "fsdp",
        scatter_dimension=1,
        tiled=True,
    ).astype(jnp.float32)
    mlp_norm = lax.rsqrt(jnp.mean(branch_mlp * branch_mlp, axis=-1, keepdims=True) + epsilon)
    layer_own = hidden + branch_mlp * mlp_norm * gain_mlp

    def whole_span(value):
        gathered = share(value.astype(low), "tp").astype(jnp.float32)
        return gathered.transpose(1, 0, 2, 3).reshape(batch_rows, local_len, width)

    grad_gain_mlp, grad_branch_mlp = norm_back(branch_mlp, mlp_norm, gain_mlp, own_cotangent)
    grad_mlp_low = lax.all_gather(grad_branch_mlp.astype(low), "fsdp", axis=1, tiled=True)
    layer_out = whole_span(layer_own)
    grad_mixed = matmul(grad_mlp_low, down_all, ((2,), (1,)))
    grad_gate_act = (
        grad_mixed * up_act * gate_sigma * (1.0 + gate_act * (1.0 - gate_sigma))
    ).astype(low)
    grad_up_act = (grad_mixed * gate_act * gate_sigma).astype(low)
    mlp_back_in = matmul(grad_gate_act, gate_all, ((2,), (1,))) + matmul(
        grad_up_act, up_all, ((2,), (1,))
    )
    grad_hidden = own_cotangent + lax.psum_scatter(
        mlp_back_in.astype(low), "fsdp", scatter_dimension=1, tiled=True
    ).astype(jnp.float32)

    hidden_flat = hidden_low.reshape(tile, width)
    grad_flat = grad_mlp_low.reshape(tile, width)

    def block_pair(value, a, b):
        flat = value.reshape(tile, -1)
        return jnp.concatenate(
            [flat[:, a * unit : (a + 1) * unit], flat[:, b * unit : (b + 1) * unit]], axis=1
        )

    grad_down_w = scatter_tp(
        matmul(block_pair(mixed_low, 0, 2), grad_flat, ((0,), (0,))),
        matmul(block_pair(mixed_low, 1, 3), grad_flat, ((0,), (0,))),
        2,
        0,
    )
    grad_gate_w = scatter_tp(
        matmul(hidden_flat, block_pair(grad_gate_act, 0, 1), ((0,), (0,))),
        matmul(hidden_flat, block_pair(grad_gate_act, 2, 3), ((0,), (0,))),
        1,
        1,
    )
    grad_up_w = scatter_tp(
        matmul(hidden_flat, block_pair(grad_up_act, 0, 2), ((0,), (0,))),
        matmul(hidden_flat, block_pair(grad_up_act, 1, 3), ((0,), (0,))),
        2,
        1,
    )
    down_back = spread(
        grad_down_w.astype(low).reshape(unit, members, rows_local).transpose(1, 0, 2), "fsdp"
    )
    grad_down = down_back.reshape(members * unit, rows_local).astype(jnp.float32)

    def unit_columns(value):
        blocks = spread(value.astype(low).reshape(members, rows_local, unit), "fsdp")
        return blocks.transpose(1, 0, 2).reshape(rows_local, members * unit).astype(jnp.float32)

    grad_gate = unit_columns(grad_gate_w)
    grad_up = unit_columns(grad_up_w)

    grad_gain_attn, grad_branch_attn = norm_back(branch_attn, attn_norm, gain_attn, grad_hidden)
    grad_attn_low = grad_branch_attn.astype(low)
    grad_attended = to_heads(matmul(grad_attn_low, out_full, ((2,), (1,))).astype(low))
    feature_blocks = jnp.concatenate(
        [
            grad_attn_low.reshape(batch_rows * sub, width),
            grad_gain_attn[None].astype(low),
            grad_gain_mlp[None].astype(low),
            jnp.zeros((14, width), low),
        ],
        axis=0,
    )
    feature_blocks = spread(
        feature_blocks.reshape(-1, members, rows_local).transpose(1, 0, 2), "fsdp"
    )
    own_features = feature_blocks[:, : batch_rows * sub].reshape(
        members, batch_rows, sub, rows_local
    )
    gain_sums = jnp.sum(
        feature_blocks[:, batch_rows * sub :].astype(jnp.float32), axis=0
    )
    attended_all = lax.all_gather(attended_low, "fsdp", axis=2, tiled=True)
    own_features = own_features.transpose(1, 0, 2, 3).reshape(batch_rows, count, rows_local)
    in_group = (group_ids[:, 0][:, None] == jnp.arange(GROUPS, dtype=jnp.int32)[None, :]).astype(
        low
    )
    out_blocks = []
    for group in range(GROUPS):
        masked = own_features * in_group[:, group][:, None, None]
        product = matmul(
            attended_all.reshape(tile, -1), masked.reshape(tile, rows_local), ((0,), (0,))
        )
        out_blocks.append(natural_rows(product.astype(low), chips))
    out_blocks.append(
        jnp.broadcast_to(gain_sums.astype(low)[None], (parts,) + gain_sums.shape)
    )
    out_sum = jnp.sum(spread(jnp.concatenate(out_blocks, axis=1), "tp").astype(jnp.float32), axis=0)
    block_rows = w_out.shape[0]
    grad_out_groups = out_sum[: GROUPS * block_rows].reshape(GROUPS, block_rows, rows_local)
    grad_out = jnp.sum(grad_out_groups, axis=0)
    grad_attn_gain = out_sum[GROUPS * block_rows]
    grad_mlp_gain = out_sum[GROUPS * block_rows + 1]

    grad_query_rot, grad_both = attend_back_tiles(
        query_low, both, grad_attended, attended, log_total, qpos, kpos, all_key_scale
    )
    grad_both = jnp.sum(spread(grad_both, "tp").astype(jnp.float32), axis=0)
    grad_qn = rotate(grad_query_rot, -1.0)
    grad_kn = rotate(grad_both[..., :pair], -1.0)
    gained_query = grad_qn * gain_query
    gained_key = grad_kn * gain_key
    cross_sums = lax.psum(
        jnp.stack(
            [jnp.sum(queries * gained_query, axis=-1), jnp.sum(keys * gained_key, axis=-1)]
        ),
        "fsdp",
    )
    grad_gain_query = jnp.sum(grad_qn * queries * query_scale, axis=(0, 1))
    grad_gain_key = jnp.sum(grad_kn * keys, axis=(0, 1))
    grad_queries = (
        query_scale * gained_query - queries * query_scale**3 * cross_sums[0][..., None] / width
    ).astype(low)
    grad_keys = (
        gained_key - keys * key_scale**2 * cross_sums[1][..., None] / width
    ).astype(low)
    grad_values = grad_both[..., pair:].astype(low)
    grad_acts = [
        jnp.concatenate(
            [
                value[..., at * 64 : at * 64 + 64]
                for value in (grad_queries, grad_keys, grad_values, jnp.zeros_like(grad_values))
            ],
            axis=-1,
        )
        for at in range(4)
    ]
    attn_back_in = sum(
        matmul(grad, piece[:width], ((2,), (1,))) for grad, piece in zip(grad_acts, weight_pieces)
    )
    input_own = grad_hidden + lax.psum_scatter(
        attn_back_in.astype(low), "fsdp", scatter_dimension=1, tiled=True
    ).astype(jnp.float32)
    input_grad = whole_span(input_own)

    token_flat = token_low.reshape(tile, width)

    def with_gain(at):
        product = matmul(token_flat, grad_acts[at].reshape(tile, bundle), ((0,), (0,)))
        gains = jnp.concatenate(
            [
                grad_gain_query[at * 64 : at * 64 + 64],
                grad_gain_key[at * 64 : at * 64 + 64],
                jnp.zeros((bundle - 2 * 64,), jnp.float32),
            ]
        )
        return jnp.concatenate(
            [product.astype(low), jnp.broadcast_to(gains[None], (16, bundle)).astype(low)], axis=0
        )

    sent = swap(jnp.stack([with_gain(2), with_gain(3)]), "fsdp", 1)
    kept = jnp.stack([with_gain(0), with_gain(1)])
    proj_blocks = jnp.where(
        core == 0, jnp.concatenate([kept, sent]), jnp.concatenate([sent, kept])
    )
    proj_sum = jnp.sum(spread(proj_blocks, "tp").astype(jnp.float32), axis=0)
    grad_query_gain = proj_sum[width, :64]
    grad_key_gain = proj_sum[width, 64:128]
    proj_back = spread(proj_sum[:width].astype(low).reshape(members, rows_local, bundle), "fsdp")

    def natural_columns(at):
        block = proj_back[:, :, at * 64 : at * 64 + 64].astype(jnp.float32)
        return block.transpose(1, 0, 2).reshape(rows_local, members * 64)

    return (
        layer_out,
        input_grad,
        natural_columns(0),
        natural_columns(1),
        natural_columns(2),
        grad_out,
        grad_query_gain,
        grad_key_gain,
        grad_attn_gain,
        grad_gate,
        grad_up,
        grad_down,
        grad_mlp_gain,
        grad_out_groups,
    )


def solution(mesh):
    in_specs = (
        P(None, "fsdp", None),
        P(None, "fsdp", None),
        P("fsdp", "tp"),
        P("fsdp", "tp"),
        P("fsdp", "tp"),
        P("tp", "fsdp"),
        P(("tp", "fsdp")),
        P(("tp", "fsdp")),
        P("fsdp"),
        P("fsdp", "tp"),
        P("fsdp", "tp"),
        P("tp", "fsdp"),
        P("fsdp"),
        P(),
        P(),
    )
    out_specs = (
        P(None, "fsdp", None),
        P(None, "fsdp", None),
        P("fsdp", "tp"),
        P("fsdp", "tp"),
        P("fsdp", "tp"),
        P("tp", "fsdp"),
        P(("tp", "fsdp")),
        P(("tp", "fsdp")),
        P("fsdp"),
        P("fsdp", "tp"),
        P("fsdp", "tp"),
        P("tp", "fsdp"),
        P("fsdp"),
        P(None, "tp", "fsdp"),
    )
    heads = 2048 // HEAD_DIM
    members, parts = mesh.shape["fsdp"], mesh.shape["tp"]
    fits = parts == 4 and heads // parts * 2 == members
    body = local_fast if fits else local
    return jax.shard_map(body, mesh=mesh, in_specs=in_specs, out_specs=out_specs, check_vma=False)
```

```python
from functools import partial

import jax
import jax.numpy as jnp
from jax import lax
from jax.experimental import pallas as pl
from jax.sharding import PartitionSpec as P

HEAD_DIM = 128
GROUPS = 2


epsilon = 1e-06
rope_base = 500000.0


def positions_of(span_order, start_row, count, span_len):
    row_index = start_row + jnp.arange(count, dtype=jnp.int32)
    span_ids = row_index // span_len
    span_table = jnp.arange(span_order.shape[0], dtype=jnp.int32)
    picked = jnp.sum(
        jnp.where(span_ids[:, None] == span_table[None, :], span_order[None, :], 0), axis=1
    )
    return picked * span_len + row_index % span_len


def rotary(inputs, positions, direction):
    half_dim = inputs.shape[-1] // 2
    inv_freq = jnp.power(
        rope_base, -(jnp.arange(half_dim, dtype=jnp.float32) * 2.0 / inputs.shape[-1])
    )
    angles = positions.astype(jnp.float32)[:, None] * inv_freq[None, :]
    cosine = jnp.cos(angles)[None, :, None, :]
    sine = direction * jnp.sin(angles)[None, :, None, :]
    front_half = inputs[..., :half_dim]
    back_half = inputs[..., half_dim:]
    return jnp.concatenate(
        [front_half * cosine - back_half * sine, back_half * cosine + front_half * sine], axis=-1
    )


def score_block(query_rot, key_rot, query_pos, key_pos):
    raw_scores = jnp.einsum(
        "rqhd,rkhd->rhqk", query_rot, key_rot, preferred_element_type=jnp.float32
    )
    scaled = raw_scores * query_rot.shape[-1] ** (-0.5)
    visible = key_pos[None, :] <= query_pos[:, None]
    return (scaled, visible)


def attend(query_rot, keys_all, values_all, query_pos, key_pos):
    scaled, visible = score_block(query_rot, keys_all, query_pos, key_pos)
    scaled = jnp.where(visible[None, None], scaled, -1e30)
    row_peak = jnp.max(scaled, axis=-1, keepdims=True)
    log_total = row_peak + jnp.log(jnp.sum(jnp.exp(scaled - row_peak), axis=-1, keepdims=True))
    attn_prob = jnp.exp(scaled - log_total).astype(jnp.bfloat16)
    attended = jnp.einsum(
        "rhqk,rkhd->rqhd", attn_prob, values_all, preferred_element_type=jnp.float32
    )
    return (attended, log_total[..., 0])


def query_step(
    carried,
    pieces,
    start_row,
    query_rot,
    grad_attended,
    log_total,
    row_delta,
    query_pos,
    span_order,
    span_len,
    skipping,
):
    key_piece, value_piece = pieces
    key_pos = positions_of(span_order, start_row, key_piece.shape[1], span_len)
    scaled, visible = score_block(query_rot, key_piece, query_pos, key_pos)
    attn_prob = jnp.where(visible[None, None], jnp.exp(scaled - log_total[..., None]), 0.0)
    grad_prob = jnp.einsum(
        "rqhd,rkhd->rhqk", grad_attended, value_piece, preferred_element_type=jnp.float32
    )
    grad_scores = (attn_prob * (grad_prob - row_delta[..., None])).astype(jnp.bfloat16)
    return jnp.einsum("rhqk,rkhd->rqhd", grad_scores, key_piece, preferred_element_type=jnp.float32)


def key_step(
    carried,
    pieces,
    start_row,
    key_rot,
    values_low,
    key_pos,
    lse_all,
    delta_all,
    span_order,
    span_len,
    skipping,
):
    query_low, grad_low = pieces
    count = query_low.shape[1]
    query_pos = positions_of(span_order, start_row, count, span_len)
    scaled, visible = score_block(query_low, key_rot, query_pos, key_pos)
    lse_rows = jnp.transpose(lse_all, (0, 2, 1))[..., None]
    delta_rows = jnp.transpose(delta_all, (0, 2, 1))[..., None]
    attn_prob = jnp.where(visible[None, None], jnp.exp(scaled - lse_rows), 0.0)
    grad_values = jnp.einsum(
        "rhqk,rqhd->rkhd",
        attn_prob.astype(jnp.bfloat16),
        grad_low,
        preferred_element_type=jnp.float32,
    )
    grad_prob = jnp.einsum(
        "rqhd,rkhd->rhqk", grad_low, values_low, preferred_element_type=jnp.float32
    )
    grad_scores = (attn_prob * (grad_prob - delta_rows)).astype(jnp.bfloat16)
    grad_keys = jnp.einsum(
        "rhqk,rqhd->rkhd", grad_scores, query_low, preferred_element_type=jnp.float32
    )
    return (grad_keys, grad_values)


def norm_back(branch, inv_root, gain, grad_output):
    gained = grad_output * gain
    grad_gain = jnp.sum(grad_output * branch * inv_root, axis=(0, 1))
    row_total = jnp.sum(branch * gained, axis=-1, keepdims=True)
    grad_branch = inv_root * gained - branch * inv_root**3 * row_total / branch.shape[-1]
    return (grad_gain, grad_branch)


def local(
    tokens,
    cotangent,
    w_query,
    w_key,
    w_value,
    w_out,
    query_gain,
    key_gain,
    attn_gain,
    w_gate,
    w_up,
    w_down,
    mlp_gain,
    group_ids,
    span_order,
):
    batch_rows, local_len, model_width = tokens.shape
    span_len = local_len // 2
    seq_len = local_len * lax.axis_size("fsdp")
    query_pos = positions_of(span_order, lax.axis_index("fsdp") * local_len, local_len, span_len)
    all_pos = positions_of(span_order, 0, seq_len, span_len)
    attn_set = (
        lax.all_gather(w_query, "fsdp", axis=0, tiled=True),
        lax.all_gather(w_key, "fsdp", axis=0, tiled=True),
        lax.all_gather(w_value, "fsdp", axis=0, tiled=True),
        lax.all_gather(w_out, "fsdp", axis=1, tiled=True),
        lax.all_gather(query_gain, "fsdp", axis=0, tiled=True),
        lax.all_gather(key_gain, "fsdp", axis=0, tiled=True),
        lax.all_gather(attn_gain, "fsdp", axis=0, tiled=True),
    )
    gain_query = attn_set[4].astype(jnp.float32)
    gain_key = attn_set[5].astype(jnp.float32)
    gain_attn = attn_set[6].astype(jnp.float32)
    tokens_low = tokens.astype(jnp.bfloat16)
    queries = jnp.einsum("rsd,de->rse", tokens_low, attn_set[0], preferred_element_type=jnp.float32)
    keys = jnp.einsum("rsd,de->rse", tokens_low, attn_set[1], preferred_element_type=jnp.float32)
    values = jnp.einsum("rsd,de->rse", tokens_low, attn_set[2], preferred_element_type=jnp.float32)
    square_sums = lax.psum(
        (jnp.sum(queries * queries, axis=-1), jnp.sum(keys * keys, axis=-1)), "tp"
    )
    query_scale = lax.rsqrt(square_sums[0] / model_width + epsilon)[..., None]
    key_scale = lax.rsqrt(square_sums[1] / model_width + epsilon)[..., None]
    local_width = queries.shape[-1]
    head_count = local_width // HEAD_DIM
    head_shape = (batch_rows, local_len, head_count, HEAD_DIM)
    query_rot = rotary(
        (queries * query_scale * gain_query).reshape(head_shape), query_pos, 1.0
    ).astype(jnp.bfloat16)
    key_rot = rotary((keys * key_scale * gain_key).reshape(head_shape), query_pos, 1.0).astype(
        jnp.bfloat16
    )
    values_low = values.astype(jnp.bfloat16).reshape(head_shape)
    keys_gathered, values_gathered = (
        lax.all_gather(key_rot, "fsdp", axis=1, tiled=True),
        lax.all_gather(values_low, "fsdp", axis=1, tiled=True),
    )
    attended, log_total = attend(query_rot, keys_gathered, values_gathered, query_pos, all_pos)
    attended_low = attended.reshape(batch_rows, local_len, local_width).astype(jnp.bfloat16)
    branch_attn = lax.psum(
        jnp.einsum(
            "rse,ed->rsd", attended_low, attn_set[3], preferred_element_type=jnp.float32
        ).astype(jnp.bfloat16),
        "tp",
    ).astype(jnp.float32)
    attn_norm = lax.rsqrt(jnp.mean(branch_attn * branch_attn, axis=-1, keepdims=True) + epsilon)
    hidden = tokens + branch_attn * attn_norm * gain_attn
    mlp_set = (
        lax.all_gather(w_gate, "fsdp", axis=0, tiled=True),
        lax.all_gather(w_up, "fsdp", axis=0, tiled=True),
        lax.all_gather(w_down, "fsdp", axis=1, tiled=True),
        lax.all_gather(mlp_gain, "fsdp", axis=0, tiled=True),
    )
    gain_mlp = mlp_set[3].astype(jnp.float32)
    hidden_low = hidden.astype(jnp.bfloat16)
    gate_act = jnp.einsum("rsd,df->rsf", hidden_low, mlp_set[0], preferred_element_type=jnp.float32)
    up_act = jnp.einsum("rsd,df->rsf", hidden_low, mlp_set[1], preferred_element_type=jnp.float32)
    mixed_low = (jax.nn.silu(gate_act) * up_act).astype(jnp.bfloat16)
    branch_mlp = lax.psum(
        jnp.einsum("rsf,fd->rsd", mixed_low, mlp_set[2], preferred_element_type=jnp.float32).astype(
            jnp.bfloat16
        ),
        "tp",
    ).astype(jnp.float32)
    mlp_norm = lax.rsqrt(jnp.mean(branch_mlp * branch_mlp, axis=-1, keepdims=True) + epsilon)
    layer_out = hidden + branch_mlp * mlp_norm * gain_mlp
    back_set = (
        lax.all_gather(w_query, "fsdp", axis=0, tiled=True),
        lax.all_gather(w_key, "fsdp", axis=0, tiled=True),
        lax.all_gather(w_value, "fsdp", axis=0, tiled=True),
        lax.all_gather(w_out, "fsdp", axis=1, tiled=True),
        lax.all_gather(w_gate, "fsdp", axis=0, tiled=True),
        lax.all_gather(w_up, "fsdp", axis=0, tiled=True),
        lax.all_gather(w_down, "fsdp", axis=1, tiled=True),
    )
    query_back, key_back, value_back, out_back, gate_back, up_back, down_back = back_set
    grad_gain_mlp, grad_branch_mlp = norm_back(branch_mlp, mlp_norm, gain_mlp, cotangent)
    grad_mlp_low = grad_branch_mlp.astype(jnp.bfloat16)
    grad_down_w = jnp.einsum(
        "rsf,rsd->fd", mixed_low, grad_mlp_low, preferred_element_type=jnp.float32
    )
    grad_mixed = jnp.einsum(
        "rsd,fd->rsf", grad_mlp_low, down_back, preferred_element_type=jnp.float32
    )
    gate_sigma = jax.nn.sigmoid(gate_act)
    grad_gate_act = (
        grad_mixed * up_act * gate_sigma * (1.0 + gate_act * (1.0 - gate_sigma))
    ).astype(jnp.bfloat16)
    grad_up_act = (grad_mixed * gate_act * gate_sigma).astype(jnp.bfloat16)
    mlp_back_in = jnp.einsum(
        "rsf,df->rsd", grad_gate_act, gate_back, preferred_element_type=jnp.float32
    ) + jnp.einsum("rsf,df->rsd", grad_up_act, up_back, preferred_element_type=jnp.float32)
    grad_hidden = cotangent + lax.psum(mlp_back_in.astype(jnp.bfloat16), "tp").astype(jnp.float32)
    grad_gate_w = jnp.einsum(
        "rsd,rsf->df", hidden_low, grad_gate_act, preferred_element_type=jnp.float32
    )
    grad_up_w = jnp.einsum(
        "rsd,rsf->df", hidden_low, grad_up_act, preferred_element_type=jnp.float32
    )
    grad_gain_attn, grad_branch_attn = norm_back(branch_attn, attn_norm, gain_attn, grad_hidden)
    grad_attn_low = grad_branch_attn.astype(jnp.bfloat16)
    per_row = jnp.einsum(
        "rse,rsd->red", attended_low, grad_attn_low, preferred_element_type=jnp.float32
    )
    member = (group_ids[:, 0][:, None] == jnp.arange(GROUPS, dtype=jnp.int32)[None, :]).astype(
        jnp.float32
    )
    grad_out_groups = jnp.sum(member[:, :, None, None] * per_row[:, None], axis=0)
    grad_out_w = jnp.sum(per_row, axis=0)
    grad_attended_low = (
        jnp.einsum("rsd,ed->rse", grad_attn_low, out_back, preferred_element_type=jnp.float32)
        .reshape(head_shape)
        .astype(jnp.bfloat16)
    )
    delta_rows = jnp.sum(grad_attended_low.astype(jnp.float32) * attended, axis=-1)
    row_delta = jnp.transpose(delta_rows, (0, 2, 1))
    zero_grad = jnp.zeros(head_shape, jnp.float32)
    query_fn = partial(
        query_step,
        query_rot=query_rot,
        grad_attended=grad_attended_low,
        log_total=log_total,
        row_delta=row_delta,
        query_pos=query_pos,
        span_order=span_order,
        span_len=span_len,
        skipping=False,
    )
    grad_query_rot = query_fn(
        zero_grad,
        (
            lax.all_gather(key_rot, "fsdp", axis=1, tiled=True),
            lax.all_gather(values_low, "fsdp", axis=1, tiled=True),
        ),
        jnp.int32(0),
    )
    lse_rows = jnp.transpose(log_total, (0, 2, 1))
    lse_all, delta_all = (
        lax.all_gather(lse_rows, "fsdp", axis=1, tiled=True),
        lax.all_gather(delta_rows, "fsdp", axis=1, tiled=True),
    )
    key_fn = partial(
        key_step,
        key_rot=key_rot,
        values_low=values_low,
        key_pos=query_pos,
        lse_all=lse_all,
        delta_all=delta_all,
        span_order=span_order,
        span_len=span_len,
        skipping=False,
    )
    grad_key_rot, grad_values = key_fn(
        (zero_grad, zero_grad),
        (
            lax.all_gather(query_rot, "fsdp", axis=1, tiled=True),
            lax.all_gather(grad_attended_low, "fsdp", axis=1, tiled=True),
        ),
        jnp.int32(0),
    )
    scaling = HEAD_DIM ** (-0.5)
    grad_qn = rotary(grad_query_rot * scaling, query_pos, -1.0).reshape(
        batch_rows, local_len, local_width
    )
    grad_kn = rotary(grad_key_rot * scaling, query_pos, -1.0).reshape(
        batch_rows, local_len, local_width
    )
    gained_query = grad_qn * gain_query
    gained_key = grad_kn * gain_key
    cross_sums = lax.psum(
        (jnp.sum(queries * gained_query, axis=-1), jnp.sum(keys * gained_key, axis=-1)), "tp"
    )
    grad_gain_query = jnp.sum(grad_qn * queries * query_scale, axis=(0, 1))
    grad_gain_key = jnp.sum(grad_kn * keys * key_scale, axis=(0, 1))
    grad_queries = (
        query_scale * gained_query
        - queries * query_scale**3 * cross_sums[0][..., None] / model_width
    ).astype(jnp.bfloat16)
    grad_keys = (
        key_scale * gained_key - keys * key_scale**3 * cross_sums[1][..., None] / model_width
    ).astype(jnp.bfloat16)
    grad_values_low = grad_values.reshape(batch_rows, local_len, local_width).astype(jnp.bfloat16)
    attn_back_in = jnp.einsum(
        "rse,de->rsd", grad_queries, query_back, preferred_element_type=jnp.float32
    )
    attn_back_in = attn_back_in + jnp.einsum(
        "rse,de->rsd", grad_keys, key_back, preferred_element_type=jnp.float32
    )
    attn_back_in = attn_back_in + jnp.einsum(
        "rse,de->rsd", grad_values_low, value_back, preferred_element_type=jnp.float32
    )
    input_grad = grad_hidden + lax.psum(attn_back_in.astype(jnp.bfloat16), "tp").astype(jnp.float32)
    grad_query_w = jnp.einsum(
        "rsd,rse->de", tokens_low, grad_queries, preferred_element_type=jnp.float32
    )
    grad_key_w = jnp.einsum(
        "rsd,rse->de", tokens_low, grad_keys, preferred_element_type=jnp.float32
    )
    grad_value_w = jnp.einsum(
        "rsd,rse->de", tokens_low, grad_values_low, preferred_element_type=jnp.float32
    )
    summed = (
        lax.psum_scatter(
            grad_query_w.astype(jnp.bfloat16), "fsdp", scatter_dimension=0, tiled=True
        ).astype(jnp.float32),
        lax.psum_scatter(
            grad_key_w.astype(jnp.bfloat16), "fsdp", scatter_dimension=0, tiled=True
        ).astype(jnp.float32),
        lax.psum_scatter(
            grad_value_w.astype(jnp.bfloat16), "fsdp", scatter_dimension=0, tiled=True
        ).astype(jnp.float32),
        lax.psum_scatter(
            grad_out_w.astype(jnp.bfloat16), "fsdp", scatter_dimension=1, tiled=True
        ).astype(jnp.float32),
        lax.psum_scatter(
            grad_out_groups.astype(jnp.bfloat16), "fsdp", scatter_dimension=2, tiled=True
        ).astype(jnp.float32),
        lax.psum_scatter(
            grad_gain_query.astype(jnp.bfloat16), "fsdp", scatter_dimension=0, tiled=True
        ).astype(jnp.float32),
        lax.psum_scatter(
            grad_gain_key.astype(jnp.bfloat16), "fsdp", scatter_dimension=0, tiled=True
        ).astype(jnp.float32),
        lax.psum_scatter(
            grad_gain_attn.astype(jnp.bfloat16), "fsdp", scatter_dimension=0, tiled=True
        ).astype(jnp.float32),
        lax.psum_scatter(
            grad_gate_w.astype(jnp.bfloat16), "fsdp", scatter_dimension=0, tiled=True
        ).astype(jnp.float32),
        lax.psum_scatter(
            grad_up_w.astype(jnp.bfloat16), "fsdp", scatter_dimension=0, tiled=True
        ).astype(jnp.float32),
        lax.psum_scatter(
            grad_down_w.astype(jnp.bfloat16), "fsdp", scatter_dimension=1, tiled=True
        ).astype(jnp.float32),
        lax.psum_scatter(
            grad_gain_mlp.astype(jnp.bfloat16), "fsdp", scatter_dimension=0, tiled=True
        ).astype(jnp.float32),
    )
    return (
        layer_out,
        input_grad,
        summed[0],
        summed[1],
        summed[2],
        summed[3],
        summed[5],
        summed[6],
        summed[7],
        summed[8],
        summed[9],
        summed[10],
        summed[11],
        summed[4],
    )


def attend_kernel(q_ref, kv_ref, qpos_ref, kpos_ref, ks_ref, out_ref, lse_ref):
    width = q_ref.shape[-1]
    head_of = (lax.broadcasted_iota(jnp.int32, (1, width), 1) // 64) % 2
    query = q_ref[0]
    qpos = qpos_ref[...]
    parts = kv_ref.shape[0]
    scaling = HEAD_DIM ** (-0.5)
    total = jnp.zeros(query.shape, jnp.float32)
    logs = []
    for head in range(2):
        picked = jnp.where(head_of == head, query, jnp.zeros_like(query))
        scores = []
        for part in range(parts):
            raw = lax.dot_general(
                picked,
                kv_ref[part, 0, :, :width],
                (((1,), (1,)), ((), ())),
                preferred_element_type=jnp.float32,
            )
            scaled = raw * (ks_ref[part, 0] * scaling)
            scores.append(jnp.where(kpos_ref[part] <= qpos, scaled, -1e30))
        peak = jnp.max(scores[0], axis=1, keepdims=True)
        for part in range(1, parts):
            peak = jnp.maximum(peak, jnp.max(scores[part], axis=1, keepdims=True))
        sums = jnp.zeros_like(peak)
        for part in range(parts):
            scores[part] = jnp.exp(scores[part] - peak)
            sums = sums + jnp.sum(scores[part], axis=1, keepdims=True)
        inverse = 1.0 / sums
        attended = jnp.zeros(query.shape, jnp.float32)
        for part in range(parts):
            attended = attended + jnp.dot(
                (scores[part] * inverse).astype(jnp.bfloat16),
                kv_ref[part, 0, :, width:],
                preferred_element_type=jnp.float32,
            )
        total = jnp.where(head_of == head, attended, total)
        logs.append(peak + jnp.log(sums))
    out_ref[0] = total
    lse_ref[0] = jnp.concatenate(logs, axis=1)


def attend_back_kernel(
    q_ref, kv_ref, grad_ref, out_ref, lse_ref, qpos_ref, kpos_ref, ks_ref, dq_ref, dkv_ref
):
    width = q_ref.shape[-1]
    head_of = (lax.broadcasted_iota(jnp.int32, (1, width), 1) // 64) % 2
    query = q_ref[0]
    grad = grad_ref[0]
    qpos = qpos_ref[...]
    parts = kv_ref.shape[0]
    scaling = HEAD_DIM ** (-0.5)
    product = grad.astype(jnp.float32) * out_ref[0]
    zero = jnp.zeros_like(query)
    queries = [jnp.where(head_of == head, query, zero) for head in range(2)]
    grads = [jnp.where(head_of == head, grad, zero) for head in range(2)]
    deltas = [
        jnp.sum(jnp.where(head_of == head, product, 0.0), axis=1, keepdims=True)
        for head in range(2)
    ]
    totals = [jnp.zeros(query.shape, jnp.float32) for _ in range(2)]
    for part in range(parts):
        key = kv_ref[part, 0, :, :width]
        value = kv_ref[part, 0, :, width:]
        visible = kpos_ref[part] <= qpos
        key_scale = ks_ref[part, 0]
        grad_key = []
        grad_value = []
        for head in range(2):
            raw = lax.dot_general(
                queries[head], key, (((1,), (1,)), ((), ())), preferred_element_type=jnp.float32
            )
            scaled = raw * (key_scale * scaling)
            prob = jnp.where(visible, jnp.exp(scaled - lse_ref[0, :, head : head + 1]), 0.0)
            grad_value.append(
                lax.dot_general(
                    prob.astype(jnp.bfloat16),
                    grad,
                    (((0,), (0,)), ((), ())),
                    preferred_element_type=jnp.float32,
                )
            )
            grad_prob = lax.dot_general(
                grads[head], value, (((1,), (1,)), ((), ())), preferred_element_type=jnp.float32
            )
            grad_scores = (prob * (grad_prob - deltas[head]) * key_scale).astype(jnp.bfloat16)
            totals[head] = totals[head] + jnp.dot(
                grad_scores, key, preferred_element_type=jnp.float32
            )
            grad_key.append(
                lax.dot_general(
                    grad_scores,
                    query,
                    (((0,), (0,)), ((), ())),
                    preferred_element_type=jnp.float32,
                )
            )
        dkv_ref[part, 0, :, :width] = (
            jnp.where(head_of == 0, grad_key[0], grad_key[1]) * scaling
        ).astype(jnp.bfloat16)
        dkv_ref[part, 0, :, width:] = jnp.where(head_of == 0, grad_value[0], grad_value[1]).astype(
            jnp.bfloat16
        )
    dq_ref[0] = jnp.where(head_of == 0, totals[0], totals[1]) * scaling


def attention_specs(rows, parts, count, width):
    row = pl.BlockSpec((1, count, width), lambda r: (r, 0, 0))
    both = pl.BlockSpec((parts, 1, count, 2 * width), lambda r: (0, r, 0, 0))
    qpos = pl.BlockSpec((count, 1), lambda r: (0, 0))
    kpos = pl.BlockSpec((parts, 1, count), lambda r: (0, 0, 0))
    scale = pl.BlockSpec((parts, 1, 1, count), lambda r: (0, r, 0, 0))
    logs = pl.BlockSpec((1, count, 2), lambda r: (r, 0, 0))
    return row, both, qpos, kpos, scale, logs


def attend_tiles(query, both, qpos, kpos, key_scale):
    rows, count, width = query.shape
    parts = both.shape[0]
    row, pair, qspec, kspec, scale, logs = attention_specs(rows, parts, count, width)
    return pl.pallas_call(
        attend_kernel,
        grid=(rows,),
        in_specs=[row, pair, qspec, kspec, scale],
        out_specs=[row, logs],
        out_shape=[
            jax.ShapeDtypeStruct((rows, count, width), jnp.float32),
            jax.ShapeDtypeStruct((rows, count, 2), jnp.float32),
        ],
        name="attend",
    )(query, both, qpos, kpos, key_scale)


def attend_back_tiles(query, both, grad, attended, log_total, qpos, kpos, key_scale):
    rows, count, width = query.shape
    parts = both.shape[0]
    row, pair, qspec, kspec, scale, logs = attention_specs(rows, parts, count, width)
    return pl.pallas_call(
        attend_back_kernel,
        grid=(rows,),
        in_specs=[row, pair, row, row, logs, qspec, kspec, scale],
        out_specs=[row, pair],
        out_shape=[
            jax.ShapeDtypeStruct((rows, count, width), jnp.float32),
            jax.ShapeDtypeStruct(both.shape, jnp.bfloat16),
        ],
        name="attend_back",
    )(query, both, grad, attended, log_total, qpos, kpos, key_scale)


def swap(value, axis, bit):
    size = lax.axis_size(axis)
    return lax.ppermute(value, axis, [(i, i ^ bit) for i in range(size)])


def spread(blocks, axis):
    return lax.all_to_all(blocks, axis, split_axis=0, concat_axis=0, tiled=True)


def others(value):
    return (value, swap(value, "tp", 1), swap(value, "tp", 2), swap(value, "tp", 3))


def in_order(pieces, part):
    odd = part % 2 == 1
    high = part // 2 == 1
    a, b, c, d = pieces
    a, b, c, d = (jnp.where(odd, p, q) for p, q in ((b, a), (a, b), (d, c), (c, d)))
    return tuple(jnp.where(high, p, q) for p, q in ((c, a), (d, b), (a, c), (b, d)))


def reduce_tp(blocks, part):
    total = lax.dynamic_index_in_dim(blocks, part, axis=0, keepdims=False).astype(jnp.float32)
    for bit in range(1, 4):
        block = lax.dynamic_index_in_dim(blocks, part ^ bit, axis=0, keepdims=False)
        total = total + swap(block, "tp", bit).astype(jnp.float32)
    return total


def tie(*values):
    return lax.optimization_barrier(values)


def gather_tp(piece, first):
    one = swap(piece, "tp", 1)
    two = swap(piece, "tp", 2)
    three = swap(one, "tp", 2) if first == 1 else swap(two, "tp", 1)
    return (piece, one, two, three)


def scatter_tp(keep, send, second, axis):
    first = 3 - second
    merged = keep + swap(send.astype(jnp.bfloat16), "tp", first).astype(jnp.float32)
    mine, other = jnp.split(merged, 2, axis=axis)
    return mine + swap(other.astype(jnp.bfloat16), "tp", second).astype(jnp.float32)


def natural_rows(grad, chips):
    width = grad.shape[-1]
    view = grad.reshape(chips, 2, 2, 2, 64, width)
    view = jnp.stack([view[:, 0], view[:, 1, ::-1]], axis=1)
    return view.transpose(1, 3, 0, 2, 4, 5).reshape(2 * 2, -1, width)


def matmul(lhs, rhs, dims):
    return lax.dot_general(lhs, rhs, (dims, ((), ())), preferred_element_type=jnp.float32)


def local_fast(
    tokens,
    cotangent,
    w_query,
    w_key,
    w_value,
    w_out,
    query_gain,
    key_gain,
    attn_gain,
    w_gate,
    w_up,
    w_down,
    mlp_gain,
    group_ids,
    span_order,
):
    low = jnp.bfloat16
    batch_rows, local_len, width = tokens.shape
    members = lax.axis_size("fsdp")
    parts = lax.axis_size("tp")
    chips = members // 2
    member = lax.axis_index("fsdp")
    part = lax.axis_index("tp")
    core = member % 2
    span_len = local_len // 2
    sub = local_len // parts
    count = members * sub
    tile = batch_rows * count
    pair = 2 * HEAD_DIM
    bundle = 4 * 64
    rows_local = w_query.shape[0]
    unit = w_gate.shape[1] // members

    own_tokens = lax.dynamic_slice_in_dim(tokens, part * sub, sub, axis=1)
    own_cotangent = lax.dynamic_slice_in_dim(cotangent, part * sub, sub, axis=1)

    def halves(weight):
        return weight.reshape(rows_local, members, 64)

    packed = jnp.concatenate(
        [halves(w_query), halves(w_key), halves(w_value), jnp.zeros_like(halves(w_value))], axis=2
    ).transpose(1, 0, 2)
    packed = spread(packed, "fsdp").reshape(width, bundle)

    def columns(weight):
        return weight.reshape(rows_local, members, unit).transpose(1, 0, 2)

    packed, gate_up = tie(packed, jnp.stack([columns(w_gate), columns(w_up)], axis=1))
    gate_up = spread(gate_up, "fsdp")
    gate_up, down = tie(gate_up, w_down.reshape(members, unit, rows_local))
    down = spread(down, "fsdp")
    gain_row = jnp.concatenate(
        [query_gain, key_gain, jnp.zeros((bundle - 2 * 64,), query_gain.dtype)]
    )
    packed = jnp.concatenate(
        [packed, jnp.broadcast_to(gain_row[None], (16, bundle)).astype(packed.dtype)], axis=0
    )
    token_low = lax.all_gather(own_tokens.astype(low), "fsdp", axis=1, tiled=True)
    cut = width // 2
    first, second = swap(packed, "tp", 1), swap(packed, "tp", 2)
    third = jnp.concatenate([swap(first[:cut], "tp", 2), swap(second[cut:], "tp", 1)], axis=0)
    near = part // 2 == core
    odd = part % 2 == 1
    mine = [jnp.where(near, packed, second), jnp.where(near, first, third)]
    theirs = [jnp.where(near, second, packed), jnp.where(near, third, first)]
    own_half = [jnp.where(odd, mine[1], mine[0]), jnp.where(odd, mine[0], mine[1])]
    other_half = swap(
        jnp.stack([jnp.where(odd, theirs[1], theirs[0]), jnp.where(odd, theirs[0], theirs[1])]),
        "fsdp",
        1,
    )

    norm_gains = jnp.concatenate(
        [attn_gain[None], mlp_gain[None], jnp.zeros((14, attn_gain.shape[0]), attn_gain.dtype)]
    )
    out_rows = lax.all_gather(
        jnp.concatenate([w_out, norm_gains.astype(w_out.dtype)], axis=0),
        "fsdp",
        axis=1,
        tiled=True,
    )
    gain_attn = out_rows[w_out.shape[0]].astype(jnp.float32)
    gain_mlp = out_rows[w_out.shape[0] + 1].astype(jnp.float32)
    out_full = lax.all_gather(
        out_rows[: w_out.shape[0]].reshape(2 * chips, 64, width), "tp", axis=1, tiled=True
    ).reshape(width, width)

    index = jnp.arange(members, dtype=jnp.int32)[:, None] * local_len
    index = (index + jnp.arange(sub, dtype=jnp.int32)[None, :]).reshape(count)
    index = index[None, :] + (part ^ jnp.arange(parts, dtype=jnp.int32))[:, None] * sub
    spans = jnp.arange(span_order.shape[0], dtype=jnp.int32)
    picked = jnp.sum(
        jnp.where((index // span_len)[..., None] == spans, span_order, 0), axis=-1
    )
    all_pos = picked * span_len + index % span_len
    query_pos = all_pos[0]
    inv_freq = jnp.power(
        rope_base, -(jnp.arange(64, dtype=jnp.float32) * 2.0 / HEAD_DIM)
    )
    angles = query_pos.astype(jnp.float32)[:, None] * jnp.tile(inv_freq, 2)[None, :]
    cosine = jnp.cos(angles)[None]
    sine = (jnp.where(core == 0, 1.0, -1.0) * jnp.sin(angles))[None]

    def rotate(value, direction):
        own, other = value[..., :HEAD_DIM], value[..., HEAD_DIM:]
        turned = direction * sine
        return jnp.concatenate(
            [own * cosine - other * turned, other * cosine + own * turned], axis=-1
        )

    weight_pieces = [own_half[0], own_half[1], other_half[0], other_half[1]]
    acts = [
        matmul(token_low, piece[:width], ((2,), (0,))) for piece in weight_pieces
    ]

    def lanes(pieces, at):
        return jnp.concatenate([piece[..., at * 64 : at * 64 + 64] for piece in pieces], axis=-1)

    queries, keys, values = (lanes(acts, at) for at in range(3))
    gain_rows = [piece[width].astype(jnp.float32) for piece in weight_pieces]
    gain_query, gain_key = lanes(gain_rows, 0), lanes(gain_rows, 1)
    key_low = rotate(keys * gain_key, 1.0).astype(low)
    both = jnp.concatenate([key_low, values.astype(low)], axis=-1)
    both, gate_up = tie(both, gate_up)
    gate_all = jnp.concatenate(gather_tp(gate_up[:, 0].reshape(width, unit), 1), axis=1)
    up_all = jnp.concatenate(gather_tp(gate_up[:, 1].reshape(width, unit), 2), axis=1)
    both = jnp.stack(others(both))
    square_sums = lax.psum(
        jnp.stack([jnp.sum(queries * queries, axis=-1), jnp.sum(keys * keys, axis=-1)]), "fsdp"
    )
    scales = lax.rsqrt(square_sums / width + epsilon)
    query_scale, key_scale = scales[0][..., None], scales[1][..., None]
    all_key_scale = jnp.stack(others(scales[1])).reshape(parts, batch_rows, 1, count)
    query_low = rotate(queries * query_scale * gain_query, 1.0).astype(low)
    qpos = query_pos[:, None]
    kpos = all_pos[:, None, :]
    attended, log_total = attend_tiles(query_low, both, qpos, kpos, all_key_scale)

    places = [(chip, half, side) for chip in range(chips) for half in range(2) for side in range(2)]

    def to_tokens(value):
        blocks = value.reshape(batch_rows, members, sub, pair).transpose(1, 0, 2, 3)
        blocks = spread(blocks, "fsdp")
        return jnp.concatenate(
            [
                blocks[2 * chip + side][..., (half ^ side) * HEAD_DIM :][..., :HEAD_DIM]
                for chip, half, side in places
            ],
            axis=-1,
        )

    def to_heads(value):
        def lanes_at(chip, half, side):
            at = places.index((chip, half, side)) * HEAD_DIM
            return value[..., at : at + HEAD_DIM]

        blocks = jnp.stack(
            [
                jnp.concatenate(
                    [lanes_at(chip, side, side), lanes_at(chip, 1 - side, side)], axis=-1
                )
                for chip in range(chips)
                for side in range(2)
            ]
        )
        return spread(blocks, "fsdp").transpose(1, 0, 2, 3).reshape(batch_rows, count, pair)

    attended_low = attended.astype(low)
    attended_low, down = tie(attended_low, down)
    down_all = jnp.concatenate(
        gather_tp(down.transpose(1, 0, 2).reshape(unit, width), 1), axis=0
    )
    branch_attn = matmul(to_tokens(attended_low), out_full, ((2,), (0,)))
    attn_norm = lax.rsqrt(jnp.mean(branch_attn * branch_attn, axis=-1, keepdims=True) + epsilon)
    hidden = own_tokens + branch_attn * attn_norm * gain_attn
    hidden_low = lax.all_gather(hidden.astype(low), "fsdp", axis=1, tiled=True)

    gate_act = matmul(hidden_low, gate_all, ((2,), (0,)))
    up_act = matmul(hidden_low, up_all, ((2,), (0,)))
    gate_sigma = jax.nn.sigmoid(gate_act)
    mixed_low = (gate_act * gate_sigma * up_act).astype(low)
    branch_mlp = lax.psum_scatter(
        matmul(mixed_low, down_all, ((2,), (0,))).astype(low),
        "fsdp",
        scatter_dimension=1,
        tiled=True,
    ).astype(jnp.float32)
    mlp_norm = lax.rsqrt(jnp.mean(branch_mlp * branch_mlp, axis=-1, keepdims=True) + epsilon)
    layer_own = hidden + branch_mlp * mlp_norm * gain_mlp

    def whole_span(value):
        pieces = in_order(others(value.astype(low)), part)
        return jnp.concatenate(pieces, axis=1).astype(jnp.float32)

    grad_gain_mlp, grad_branch_mlp = norm_back(branch_mlp, mlp_norm, gain_mlp, own_cotangent)
    grad_mlp_low = lax.all_gather(grad_branch_mlp.astype(low), "fsdp", axis=1, tiled=True)
    layer_out = whole_span(layer_own)
    grad_mixed = matmul(grad_mlp_low, down_all, ((2,), (1,)))
    grad_gate_act = (
        grad_mixed * up_act * gate_sigma * (1.0 + gate_act * (1.0 - gate_sigma))
    ).astype(low)
    grad_up_act = (grad_mixed * gate_act * gate_sigma).astype(low)
    mlp_back_in = matmul(grad_gate_act, gate_all, ((2,), (1,))) + matmul(
        grad_up_act, up_all, ((2,), (1,))
    )
    grad_hidden = own_cotangent + lax.psum_scatter(
        mlp_back_in.astype(low), "fsdp", scatter_dimension=1, tiled=True
    ).astype(jnp.float32)

    hidden_flat = hidden_low.reshape(tile, width)
    grad_flat = grad_mlp_low.reshape(tile, width)

    def block_pair(value, a, b):
        flat = value.reshape(tile, -1)
        return jnp.concatenate(
            [flat[:, a * unit : (a + 1) * unit], flat[:, b * unit : (b + 1) * unit]], axis=1
        )

    grad_down_w = scatter_tp(
        matmul(block_pair(mixed_low, 0, 2), grad_flat, ((0,), (0,))),
        matmul(block_pair(mixed_low, 1, 3), grad_flat, ((0,), (0,))),
        2,
        0,
    )
    grad_gate_w = scatter_tp(
        matmul(hidden_flat, block_pair(grad_gate_act, 0, 1), ((0,), (0,))),
        matmul(hidden_flat, block_pair(grad_gate_act, 2, 3), ((0,), (0,))),
        1,
        1,
    )
    grad_up_w = scatter_tp(
        matmul(hidden_flat, block_pair(grad_up_act, 0, 2), ((0,), (0,))),
        matmul(hidden_flat, block_pair(grad_up_act, 1, 3), ((0,), (0,))),
        2,
        1,
    )
    down_back = spread(
        grad_down_w.astype(low).reshape(unit, members, rows_local).transpose(1, 0, 2), "fsdp"
    )

    def unit_back(value):
        return spread(value.astype(low).reshape(members, rows_local, unit), "fsdp")

    def unit_columns(blocks):
        return blocks.transpose(1, 0, 2).reshape(rows_local, members * unit).astype(jnp.float32)

    gate_back = unit_back(grad_gate_w)
    up_back = unit_back(grad_up_w)

    grad_gain_attn, grad_branch_attn = norm_back(branch_attn, attn_norm, gain_attn, grad_hidden)
    grad_attn_low = grad_branch_attn.astype(low)
    grad_attended = to_heads(matmul(grad_attn_low, out_full, ((2,), (1,))).astype(low))
    feature_blocks = jnp.concatenate(
        [
            grad_attn_low.reshape(batch_rows * sub, width),
            grad_gain_attn[None].astype(low),
            grad_gain_mlp[None].astype(low),
            jnp.zeros((14, width), low),
        ],
        axis=0,
    )
    feature_blocks = spread(
        feature_blocks.reshape(-1, members, rows_local).transpose(1, 0, 2), "fsdp"
    )
    own_features = feature_blocks[:, : batch_rows * sub].reshape(
        members, batch_rows, sub, rows_local
    )
    gain_sums = jnp.sum(
        feature_blocks[:, batch_rows * sub :].astype(jnp.float32), axis=0
    )
    attended_all = lax.all_gather(attended_low, "fsdp", axis=2, tiled=True)
    own_features = own_features.transpose(1, 0, 2, 3).reshape(batch_rows, count, rows_local)
    in_group = (group_ids[:, 0][:, None] == jnp.arange(GROUPS, dtype=jnp.int32)[None, :]).astype(
        low
    )
    out_blocks = []
    for group in range(GROUPS):
        masked = own_features * in_group[:, group][:, None, None]
        product = matmul(
            attended_all.reshape(tile, -1), masked.reshape(tile, rows_local), ((0,), (0,))
        )
        out_blocks.append(natural_rows(product.astype(low), chips))
    out_blocks.append(
        jnp.broadcast_to(gain_sums.astype(low)[None], (parts,) + gain_sums.shape)
    )
    out_sum = reduce_tp(jnp.concatenate(out_blocks, axis=1), part)
    block_rows = w_out.shape[0]
    grad_out_groups = out_sum[: GROUPS * block_rows].reshape(GROUPS, block_rows, rows_local)
    grad_out = jnp.sum(grad_out_groups, axis=0)
    grad_attn_gain = out_sum[GROUPS * block_rows]
    grad_mlp_gain = out_sum[GROUPS * block_rows + 1]

    grad_query_rot, grad_both = attend_back_tiles(
        query_low, both, grad_attended, attended, log_total, qpos, kpos, all_key_scale
    )
    grad_both = sum(
        value.astype(jnp.float32)
        for value in [grad_both[0]] + [swap(grad_both[bit], "tp", bit) for bit in range(1, 4)]
    )
    grad_qn = rotate(grad_query_rot, -1.0)
    grad_kn = rotate(grad_both[..., :pair], -1.0)
    gained_query = grad_qn * gain_query
    gained_key = grad_kn * gain_key
    cross_sums = lax.psum(
        jnp.stack(
            [jnp.sum(queries * gained_query, axis=-1), jnp.sum(keys * gained_key, axis=-1)]
        ),
        "fsdp",
    )
    grad_gain_query = jnp.sum(grad_qn * queries * query_scale, axis=(0, 1))
    grad_gain_key = jnp.sum(grad_kn * keys, axis=(0, 1))
    grad_queries = (
        query_scale * gained_query - queries * query_scale**3 * cross_sums[0][..., None] / width
    ).astype(low)
    grad_keys = (
        gained_key - keys * key_scale**2 * cross_sums[1][..., None] / width
    ).astype(low)
    grad_values = grad_both[..., pair:].astype(low)
    grad_acts = [
        jnp.concatenate(
            [
                value[..., at * 64 : at * 64 + 64]
                for value in (grad_queries, grad_keys, grad_values, jnp.zeros_like(grad_values))
            ],
            axis=-1,
        )
        for at in range(4)
    ]
    attn_back_in = sum(
        matmul(grad, piece[:width], ((2,), (1,))) for grad, piece in zip(grad_acts, weight_pieces)
    )
    attn_back_low, down_back, gate_back = tie(attn_back_in.astype(low), down_back, gate_back)
    grad_down = down_back.reshape(members * unit, rows_local).astype(jnp.float32)
    grad_gate = unit_columns(gate_back)
    input_own = grad_hidden + lax.psum_scatter(
        attn_back_low, "fsdp", scatter_dimension=1, tiled=True
    ).astype(jnp.float32)
    input_grad = whole_span(input_own)

    token_flat = token_low.reshape(tile, width)

    def with_gain(at):
        product = matmul(token_flat, grad_acts[at].reshape(tile, bundle), ((0,), (0,)))
        gains = jnp.concatenate(
            [
                grad_gain_query[at * 64 : at * 64 + 64],
                grad_gain_key[at * 64 : at * 64 + 64],
                jnp.zeros((bundle - 2 * 64,), jnp.float32),
            ]
        )
        return jnp.concatenate(
            [product.astype(low), jnp.broadcast_to(gains[None], (16, bundle)).astype(low)], axis=0
        )

    sent = swap(jnp.stack([with_gain(2), with_gain(3)]), "fsdp", 1)
    kept = jnp.stack([with_gain(0), with_gain(1)])
    proj_blocks = jnp.where(
        core == 0, jnp.concatenate([kept, sent]), jnp.concatenate([sent, kept])
    )
    proj_sum = reduce_tp(proj_blocks, part)
    grad_query_gain = proj_sum[width, :64]
    grad_key_gain = proj_sum[width, 64:128]
    proj_low, up_back = tie(proj_sum[:width].astype(low), up_back)
    grad_up = unit_columns(up_back)
    proj_back = spread(proj_low.reshape(members, rows_local, bundle), "fsdp")

    def natural_columns(at):
        block = proj_back[:, :, at * 64 : at * 64 + 64].astype(jnp.float32)
        return block.transpose(1, 0, 2).reshape(rows_local, members * 64)

    return (
        layer_out,
        input_grad,
        natural_columns(0),
        natural_columns(1),
        natural_columns(2),
        grad_out,
        grad_query_gain,
        grad_key_gain,
        grad_attn_gain,
        grad_gate,
        grad_up,
        grad_down,
        grad_mlp_gain,
        grad_out_groups,
    )


def solution(mesh):
    in_specs = (
        P(None, "fsdp", None),
        P(None, "fsdp", None),
        P("fsdp", "tp"),
        P("fsdp", "tp"),
        P("fsdp", "tp"),
        P("tp", "fsdp"),
        P(("tp", "fsdp")),
        P(("tp", "fsdp")),
        P("fsdp"),
        P("fsdp", "tp"),
        P("fsdp", "tp"),
        P("tp", "fsdp"),
        P("fsdp"),
        P(),
        P(),
    )
    out_specs = (
        P(None, "fsdp", None),
        P(None, "fsdp", None),
        P("fsdp", "tp"),
        P("fsdp", "tp"),
        P("fsdp", "tp"),
        P("tp", "fsdp"),
        P(("tp", "fsdp")),
        P(("tp", "fsdp")),
        P("fsdp"),
        P("fsdp", "tp"),
        P("fsdp", "tp"),
        P("tp", "fsdp"),
        P("fsdp"),
        P(None, "tp", "fsdp"),
    )
    heads = 2048 // HEAD_DIM
    members, parts = mesh.shape["fsdp"], mesh.shape["tp"]
    fits = parts == 4 and heads // parts * 2 == members
    body = local_fast if fits else local
    return jax.shard_map(body, mesh=mesh, in_specs=in_specs, out_specs=out_specs, check_vma=False)
```

```python
from functools import partial

import jax
import jax.numpy as jnp
from jax import lax
from jax.experimental import pallas as pl
from jax.sharding import PartitionSpec as P

HEAD_DIM = 128
GROUPS = 2


epsilon = 1e-06
rope_base = 500000.0


def positions_of(span_order, start_row, count, span_len):
    row_index = start_row + jnp.arange(count, dtype=jnp.int32)
    span_ids = row_index // span_len
    span_table = jnp.arange(span_order.shape[0], dtype=jnp.int32)
    picked = jnp.sum(
        jnp.where(span_ids[:, None] == span_table[None, :], span_order[None, :], 0), axis=1
    )
    return picked * span_len + row_index % span_len


def rotary(inputs, positions, direction):
    half_dim = inputs.shape[-1] // 2
    inv_freq = jnp.power(
        rope_base, -(jnp.arange(half_dim, dtype=jnp.float32) * 2.0 / inputs.shape[-1])
    )
    angles = positions.astype(jnp.float32)[:, None] * inv_freq[None, :]
    cosine = jnp.cos(angles)[None, :, None, :]
    sine = direction * jnp.sin(angles)[None, :, None, :]
    front_half = inputs[..., :half_dim]
    back_half = inputs[..., half_dim:]
    return jnp.concatenate(
        [front_half * cosine - back_half * sine, back_half * cosine + front_half * sine], axis=-1
    )


def score_block(query_rot, key_rot, query_pos, key_pos):
    raw_scores = jnp.einsum(
        "rqhd,rkhd->rhqk", query_rot, key_rot, preferred_element_type=jnp.float32
    )
    scaled = raw_scores * query_rot.shape[-1] ** (-0.5)
    visible = key_pos[None, :] <= query_pos[:, None]
    return (scaled, visible)


def attend(query_rot, keys_all, values_all, query_pos, key_pos):
    scaled, visible = score_block(query_rot, keys_all, query_pos, key_pos)
    scaled = jnp.where(visible[None, None], scaled, -1e30)
    row_peak = jnp.max(scaled, axis=-1, keepdims=True)
    log_total = row_peak + jnp.log(jnp.sum(jnp.exp(scaled - row_peak), axis=-1, keepdims=True))
    attn_prob = jnp.exp(scaled - log_total).astype(jnp.bfloat16)
    attended = jnp.einsum(
        "rhqk,rkhd->rqhd", attn_prob, values_all, preferred_element_type=jnp.float32
    )
    return (attended, log_total[..., 0])


def query_step(
    carried,
    pieces,
    start_row,
    query_rot,
    grad_attended,
    log_total,
    row_delta,
    query_pos,
    span_order,
    span_len,
    skipping,
):
    key_piece, value_piece = pieces
    key_pos = positions_of(span_order, start_row, key_piece.shape[1], span_len)
    scaled, visible = score_block(query_rot, key_piece, query_pos, key_pos)
    attn_prob = jnp.where(visible[None, None], jnp.exp(scaled - log_total[..., None]), 0.0)
    grad_prob = jnp.einsum(
        "rqhd,rkhd->rhqk", grad_attended, value_piece, preferred_element_type=jnp.float32
    )
    grad_scores = (attn_prob * (grad_prob - row_delta[..., None])).astype(jnp.bfloat16)
    return jnp.einsum("rhqk,rkhd->rqhd", grad_scores, key_piece, preferred_element_type=jnp.float32)


def key_step(
    carried,
    pieces,
    start_row,
    key_rot,
    values_low,
    key_pos,
    lse_all,
    delta_all,
    span_order,
    span_len,
    skipping,
):
    query_low, grad_low = pieces
    count = query_low.shape[1]
    query_pos = positions_of(span_order, start_row, count, span_len)
    scaled, visible = score_block(query_low, key_rot, query_pos, key_pos)
    lse_rows = jnp.transpose(lse_all, (0, 2, 1))[..., None]
    delta_rows = jnp.transpose(delta_all, (0, 2, 1))[..., None]
    attn_prob = jnp.where(visible[None, None], jnp.exp(scaled - lse_rows), 0.0)
    grad_values = jnp.einsum(
        "rhqk,rqhd->rkhd",
        attn_prob.astype(jnp.bfloat16),
        grad_low,
        preferred_element_type=jnp.float32,
    )
    grad_prob = jnp.einsum(
        "rqhd,rkhd->rhqk", grad_low, values_low, preferred_element_type=jnp.float32
    )
    grad_scores = (attn_prob * (grad_prob - delta_rows)).astype(jnp.bfloat16)
    grad_keys = jnp.einsum(
        "rhqk,rqhd->rkhd", grad_scores, query_low, preferred_element_type=jnp.float32
    )
    return (grad_keys, grad_values)


def norm_back(branch, inv_root, gain, grad_output):
    gained = grad_output * gain
    grad_gain = jnp.sum(grad_output * branch * inv_root, axis=(0, 1))
    row_total = jnp.sum(branch * gained, axis=-1, keepdims=True)
    grad_branch = inv_root * gained - branch * inv_root**3 * row_total / branch.shape[-1]
    return (grad_gain, grad_branch)


def local(
    tokens,
    cotangent,
    w_query,
    w_key,
    w_value,
    w_out,
    query_gain,
    key_gain,
    attn_gain,
    w_gate,
    w_up,
    w_down,
    mlp_gain,
    group_ids,
    span_order,
):
    batch_rows, local_len, model_width = tokens.shape
    span_len = local_len // 2
    seq_len = local_len * lax.axis_size("fsdp")
    query_pos = positions_of(span_order, lax.axis_index("fsdp") * local_len, local_len, span_len)
    all_pos = positions_of(span_order, 0, seq_len, span_len)
    attn_set = (
        lax.all_gather(w_query, "fsdp", axis=0, tiled=True),
        lax.all_gather(w_key, "fsdp", axis=0, tiled=True),
        lax.all_gather(w_value, "fsdp", axis=0, tiled=True),
        lax.all_gather(w_out, "fsdp", axis=1, tiled=True),
        lax.all_gather(query_gain, "fsdp", axis=0, tiled=True),
        lax.all_gather(key_gain, "fsdp", axis=0, tiled=True),
        lax.all_gather(attn_gain, "fsdp", axis=0, tiled=True),
    )
    gain_query = attn_set[4].astype(jnp.float32)
    gain_key = attn_set[5].astype(jnp.float32)
    gain_attn = attn_set[6].astype(jnp.float32)
    tokens_low = tokens.astype(jnp.bfloat16)
    queries = jnp.einsum("rsd,de->rse", tokens_low, attn_set[0], preferred_element_type=jnp.float32)
    keys = jnp.einsum("rsd,de->rse", tokens_low, attn_set[1], preferred_element_type=jnp.float32)
    values = jnp.einsum("rsd,de->rse", tokens_low, attn_set[2], preferred_element_type=jnp.float32)
    square_sums = lax.psum(
        (jnp.sum(queries * queries, axis=-1), jnp.sum(keys * keys, axis=-1)), "tp"
    )
    query_scale = lax.rsqrt(square_sums[0] / model_width + epsilon)[..., None]
    key_scale = lax.rsqrt(square_sums[1] / model_width + epsilon)[..., None]
    local_width = queries.shape[-1]
    head_count = local_width // HEAD_DIM
    head_shape = (batch_rows, local_len, head_count, HEAD_DIM)
    query_rot = rotary(
        (queries * query_scale * gain_query).reshape(head_shape), query_pos, 1.0
    ).astype(jnp.bfloat16)
    key_rot = rotary((keys * key_scale * gain_key).reshape(head_shape), query_pos, 1.0).astype(
        jnp.bfloat16
    )
    values_low = values.astype(jnp.bfloat16).reshape(head_shape)
    keys_gathered, values_gathered = (
        lax.all_gather(key_rot, "fsdp", axis=1, tiled=True),
        lax.all_gather(values_low, "fsdp", axis=1, tiled=True),
    )
    attended, log_total = attend(query_rot, keys_gathered, values_gathered, query_pos, all_pos)
    attended_low = attended.reshape(batch_rows, local_len, local_width).astype(jnp.bfloat16)
    branch_attn = lax.psum(
        jnp.einsum(
            "rse,ed->rsd", attended_low, attn_set[3], preferred_element_type=jnp.float32
        ).astype(jnp.bfloat16),
        "tp",
    ).astype(jnp.float32)
    attn_norm = lax.rsqrt(jnp.mean(branch_attn * branch_attn, axis=-1, keepdims=True) + epsilon)
    hidden = tokens + branch_attn * attn_norm * gain_attn
    mlp_set = (
        lax.all_gather(w_gate, "fsdp", axis=0, tiled=True),
        lax.all_gather(w_up, "fsdp", axis=0, tiled=True),
        lax.all_gather(w_down, "fsdp", axis=1, tiled=True),
        lax.all_gather(mlp_gain, "fsdp", axis=0, tiled=True),
    )
    gain_mlp = mlp_set[3].astype(jnp.float32)
    hidden_low = hidden.astype(jnp.bfloat16)
    gate_act = jnp.einsum("rsd,df->rsf", hidden_low, mlp_set[0], preferred_element_type=jnp.float32)
    up_act = jnp.einsum("rsd,df->rsf", hidden_low, mlp_set[1], preferred_element_type=jnp.float32)
    mixed_low = (jax.nn.silu(gate_act) * up_act).astype(jnp.bfloat16)
    branch_mlp = lax.psum(
        jnp.einsum("rsf,fd->rsd", mixed_low, mlp_set[2], preferred_element_type=jnp.float32).astype(
            jnp.bfloat16
        ),
        "tp",
    ).astype(jnp.float32)
    mlp_norm = lax.rsqrt(jnp.mean(branch_mlp * branch_mlp, axis=-1, keepdims=True) + epsilon)
    layer_out = hidden + branch_mlp * mlp_norm * gain_mlp
    back_set = (
        lax.all_gather(w_query, "fsdp", axis=0, tiled=True),
        lax.all_gather(w_key, "fsdp", axis=0, tiled=True),
        lax.all_gather(w_value, "fsdp", axis=0, tiled=True),
        lax.all_gather(w_out, "fsdp", axis=1, tiled=True),
        lax.all_gather(w_gate, "fsdp", axis=0, tiled=True),
        lax.all_gather(w_up, "fsdp", axis=0, tiled=True),
        lax.all_gather(w_down, "fsdp", axis=1, tiled=True),
    )
    query_back, key_back, value_back, out_back, gate_back, up_back, down_back = back_set
    grad_gain_mlp, grad_branch_mlp = norm_back(branch_mlp, mlp_norm, gain_mlp, cotangent)
    grad_mlp_low = grad_branch_mlp.astype(jnp.bfloat16)
    grad_down_w = jnp.einsum(
        "rsf,rsd->fd", mixed_low, grad_mlp_low, preferred_element_type=jnp.float32
    )
    grad_mixed = jnp.einsum(
        "rsd,fd->rsf", grad_mlp_low, down_back, preferred_element_type=jnp.float32
    )
    gate_sigma = jax.nn.sigmoid(gate_act)
    grad_gate_act = (
        grad_mixed * up_act * gate_sigma * (1.0 + gate_act * (1.0 - gate_sigma))
    ).astype(jnp.bfloat16)
    grad_up_act = (grad_mixed * gate_act * gate_sigma).astype(jnp.bfloat16)
    mlp_back_in = jnp.einsum(
        "rsf,df->rsd", grad_gate_act, gate_back, preferred_element_type=jnp.float32
    ) + jnp.einsum("rsf,df->rsd", grad_up_act, up_back, preferred_element_type=jnp.float32)
    grad_hidden = cotangent + lax.psum(mlp_back_in.astype(jnp.bfloat16), "tp").astype(jnp.float32)
    grad_gate_w = jnp.einsum(
        "rsd,rsf->df", hidden_low, grad_gate_act, preferred_element_type=jnp.float32
    )
    grad_up_w = jnp.einsum(
        "rsd,rsf->df", hidden_low, grad_up_act, preferred_element_type=jnp.float32
    )
    grad_gain_attn, grad_branch_attn = norm_back(branch_attn, attn_norm, gain_attn, grad_hidden)
    grad_attn_low = grad_branch_attn.astype(jnp.bfloat16)
    per_row = jnp.einsum(
        "rse,rsd->red", attended_low, grad_attn_low, preferred_element_type=jnp.float32
    )
    member = (group_ids[:, 0][:, None] == jnp.arange(GROUPS, dtype=jnp.int32)[None, :]).astype(
        jnp.float32
    )
    grad_out_groups = jnp.sum(member[:, :, None, None] * per_row[:, None], axis=0)
    grad_out_w = jnp.sum(per_row, axis=0)
    grad_attended_low = (
        jnp.einsum("rsd,ed->rse", grad_attn_low, out_back, preferred_element_type=jnp.float32)
        .reshape(head_shape)
        .astype(jnp.bfloat16)
    )
    delta_rows = jnp.sum(grad_attended_low.astype(jnp.float32) * attended, axis=-1)
    row_delta = jnp.transpose(delta_rows, (0, 2, 1))
    zero_grad = jnp.zeros(head_shape, jnp.float32)
    query_fn = partial(
        query_step,
        query_rot=query_rot,
        grad_attended=grad_attended_low,
        log_total=log_total,
        row_delta=row_delta,
        query_pos=query_pos,
        span_order=span_order,
        span_len=span_len,
        skipping=False,
    )
    grad_query_rot = query_fn(
        zero_grad,
        (
            lax.all_gather(key_rot, "fsdp", axis=1, tiled=True),
            lax.all_gather(values_low, "fsdp", axis=1, tiled=True),
        ),
        jnp.int32(0),
    )
    lse_rows = jnp.transpose(log_total, (0, 2, 1))
    lse_all, delta_all = (
        lax.all_gather(lse_rows, "fsdp", axis=1, tiled=True),
        lax.all_gather(delta_rows, "fsdp", axis=1, tiled=True),
    )
    key_fn = partial(
        key_step,
        key_rot=key_rot,
        values_low=values_low,
        key_pos=query_pos,
        lse_all=lse_all,
        delta_all=delta_all,
        span_order=span_order,
        span_len=span_len,
        skipping=False,
    )
    grad_key_rot, grad_values = key_fn(
        (zero_grad, zero_grad),
        (
            lax.all_gather(query_rot, "fsdp", axis=1, tiled=True),
            lax.all_gather(grad_attended_low, "fsdp", axis=1, tiled=True),
        ),
        jnp.int32(0),
    )
    scaling = HEAD_DIM ** (-0.5)
    grad_qn = rotary(grad_query_rot * scaling, query_pos, -1.0).reshape(
        batch_rows, local_len, local_width
    )
    grad_kn = rotary(grad_key_rot * scaling, query_pos, -1.0).reshape(
        batch_rows, local_len, local_width
    )
    gained_query = grad_qn * gain_query
    gained_key = grad_kn * gain_key
    cross_sums = lax.psum(
        (jnp.sum(queries * gained_query, axis=-1), jnp.sum(keys * gained_key, axis=-1)), "tp"
    )
    grad_gain_query = jnp.sum(grad_qn * queries * query_scale, axis=(0, 1))
    grad_gain_key = jnp.sum(grad_kn * keys * key_scale, axis=(0, 1))
    grad_queries = (
        query_scale * gained_query
        - queries * query_scale**3 * cross_sums[0][..., None] / model_width
    ).astype(jnp.bfloat16)
    grad_keys = (
        key_scale * gained_key - keys * key_scale**3 * cross_sums[1][..., None] / model_width
    ).astype(jnp.bfloat16)
    grad_values_low = grad_values.reshape(batch_rows, local_len, local_width).astype(jnp.bfloat16)
    attn_back_in = jnp.einsum(
        "rse,de->rsd", grad_queries, query_back, preferred_element_type=jnp.float32
    )
    attn_back_in = attn_back_in + jnp.einsum(
        "rse,de->rsd", grad_keys, key_back, preferred_element_type=jnp.float32
    )
    attn_back_in = attn_back_in + jnp.einsum(
        "rse,de->rsd", grad_values_low, value_back, preferred_element_type=jnp.float32
    )
    input_grad = grad_hidden + lax.psum(attn_back_in.astype(jnp.bfloat16), "tp").astype(jnp.float32)
    grad_query_w = jnp.einsum(
        "rsd,rse->de", tokens_low, grad_queries, preferred_element_type=jnp.float32
    )
    grad_key_w = jnp.einsum(
        "rsd,rse->de", tokens_low, grad_keys, preferred_element_type=jnp.float32
    )
    grad_value_w = jnp.einsum(
        "rsd,rse->de", tokens_low, grad_values_low, preferred_element_type=jnp.float32
    )
    summed = (
        lax.psum_scatter(
            grad_query_w.astype(jnp.bfloat16), "fsdp", scatter_dimension=0, tiled=True
        ).astype(jnp.float32),
        lax.psum_scatter(
            grad_key_w.astype(jnp.bfloat16), "fsdp", scatter_dimension=0, tiled=True
        ).astype(jnp.float32),
        lax.psum_scatter(
            grad_value_w.astype(jnp.bfloat16), "fsdp", scatter_dimension=0, tiled=True
        ).astype(jnp.float32),
        lax.psum_scatter(
            grad_out_w.astype(jnp.bfloat16), "fsdp", scatter_dimension=1, tiled=True
        ).astype(jnp.float32),
        lax.psum_scatter(
            grad_out_groups.astype(jnp.bfloat16), "fsdp", scatter_dimension=2, tiled=True
        ).astype(jnp.float32),
        lax.psum_scatter(
            grad_gain_query.astype(jnp.bfloat16), "fsdp", scatter_dimension=0, tiled=True
        ).astype(jnp.float32),
        lax.psum_scatter(
            grad_gain_key.astype(jnp.bfloat16), "fsdp", scatter_dimension=0, tiled=True
        ).astype(jnp.float32),
        lax.psum_scatter(
            grad_gain_attn.astype(jnp.bfloat16), "fsdp", scatter_dimension=0, tiled=True
        ).astype(jnp.float32),
        lax.psum_scatter(
            grad_gate_w.astype(jnp.bfloat16), "fsdp", scatter_dimension=0, tiled=True
        ).astype(jnp.float32),
        lax.psum_scatter(
            grad_up_w.astype(jnp.bfloat16), "fsdp", scatter_dimension=0, tiled=True
        ).astype(jnp.float32),
        lax.psum_scatter(
            grad_down_w.astype(jnp.bfloat16), "fsdp", scatter_dimension=1, tiled=True
        ).astype(jnp.float32),
        lax.psum_scatter(
            grad_gain_mlp.astype(jnp.bfloat16), "fsdp", scatter_dimension=0, tiled=True
        ).astype(jnp.float32),
    )
    return (
        layer_out,
        input_grad,
        summed[0],
        summed[1],
        summed[2],
        summed[3],
        summed[5],
        summed[6],
        summed[7],
        summed[8],
        summed[9],
        summed[10],
        summed[11],
        summed[4],
    )


def attend_kernel(q_ref, kv_ref, qpos_ref, kpos_ref, ks_ref, out_ref, lse_ref):
    width = q_ref.shape[-1]
    head_of = (lax.broadcasted_iota(jnp.int32, (1, width), 1) // 64) % 2
    query = q_ref[0]
    qpos = qpos_ref[...]
    parts = kv_ref.shape[0]
    scaling = HEAD_DIM ** (-0.5)
    total = jnp.zeros(query.shape, jnp.float32)
    logs = []
    for head in range(2):
        picked = jnp.where(head_of == head, query, jnp.zeros_like(query))
        scores = []
        for part in range(parts):
            raw = lax.dot_general(
                picked,
                kv_ref[part, 0, :, :width],
                (((1,), (1,)), ((), ())),
                preferred_element_type=jnp.float32,
            )
            scaled = raw * (ks_ref[part, 0] * scaling)
            scores.append(jnp.where(kpos_ref[part] <= qpos, scaled, -1e30))
        peak = jnp.max(scores[0], axis=1, keepdims=True)
        for part in range(1, parts):
            peak = jnp.maximum(peak, jnp.max(scores[part], axis=1, keepdims=True))
        sums = jnp.zeros_like(peak)
        for part in range(parts):
            scores[part] = jnp.exp(scores[part] - peak)
            sums = sums + jnp.sum(scores[part], axis=1, keepdims=True)
        inverse = 1.0 / sums
        attended = jnp.zeros(query.shape, jnp.float32)
        for part in range(parts):
            attended = attended + jnp.dot(
                (scores[part] * inverse).astype(jnp.bfloat16),
                kv_ref[part, 0, :, width:],
                preferred_element_type=jnp.float32,
            )
        total = jnp.where(head_of == head, attended, total)
        logs.append(peak + jnp.log(sums))
    out_ref[0] = total
    lse_ref[0] = jnp.concatenate(logs, axis=1)


def attend_back_kernel(
    q_ref, kv_ref, grad_ref, out_ref, lse_ref, qpos_ref, kpos_ref, ks_ref, dq_ref, dkv_ref
):
    width = q_ref.shape[-1]
    head_of = (lax.broadcasted_iota(jnp.int32, (1, width), 1) // 64) % 2
    query = q_ref[0]
    grad = grad_ref[0]
    qpos = qpos_ref[...]
    parts = kv_ref.shape[0]
    scaling = HEAD_DIM ** (-0.5)
    product = grad.astype(jnp.float32) * out_ref[0]
    zero = jnp.zeros_like(query)
    queries = [jnp.where(head_of == head, query, zero) for head in range(2)]
    grads = [jnp.where(head_of == head, grad, zero) for head in range(2)]
    deltas = [
        jnp.sum(jnp.where(head_of == head, product, 0.0), axis=1, keepdims=True)
        for head in range(2)
    ]
    totals = [jnp.zeros(query.shape, jnp.float32) for _ in range(2)]
    for part in range(parts):
        key = kv_ref[part, 0, :, :width]
        value = kv_ref[part, 0, :, width:]
        visible = kpos_ref[part] <= qpos
        key_scale = ks_ref[part, 0]
        grad_key = []
        grad_value = []
        for head in range(2):
            raw = lax.dot_general(
                queries[head], key, (((1,), (1,)), ((), ())), preferred_element_type=jnp.float32
            )
            scaled = raw * (key_scale * scaling)
            prob = jnp.where(visible, jnp.exp(scaled - lse_ref[0, :, head : head + 1]), 0.0)
            grad_value.append(
                lax.dot_general(
                    prob.astype(jnp.bfloat16),
                    grad,
                    (((0,), (0,)), ((), ())),
                    preferred_element_type=jnp.float32,
                )
            )
            grad_prob = lax.dot_general(
                grads[head], value, (((1,), (1,)), ((), ())), preferred_element_type=jnp.float32
            )
            grad_scores = (prob * (grad_prob - deltas[head]) * key_scale).astype(jnp.bfloat16)
            totals[head] = totals[head] + jnp.dot(
                grad_scores, key, preferred_element_type=jnp.float32
            )
            grad_key.append(
                lax.dot_general(
                    grad_scores,
                    query,
                    (((0,), (0,)), ((), ())),
                    preferred_element_type=jnp.float32,
                )
            )
        dkv_ref[part, 0, :, :width] = (
            jnp.where(head_of == 0, grad_key[0], grad_key[1]) * scaling
        ).astype(jnp.bfloat16)
        dkv_ref[part, 0, :, width:] = jnp.where(head_of == 0, grad_value[0], grad_value[1]).astype(
            jnp.bfloat16
        )
    dq_ref[0] = jnp.where(head_of == 0, totals[0], totals[1]) * scaling


def attention_specs(rows, parts, count, width):
    row = pl.BlockSpec((1, count, width), lambda r: (r, 0, 0))
    both = pl.BlockSpec((parts, 1, count, 2 * width), lambda r: (0, r, 0, 0))
    qpos = pl.BlockSpec((count, 1), lambda r: (0, 0))
    kpos = pl.BlockSpec((parts, 1, count), lambda r: (0, 0, 0))
    scale = pl.BlockSpec((parts, 1, 1, count), lambda r: (0, r, 0, 0))
    logs = pl.BlockSpec((1, count, 2), lambda r: (r, 0, 0))
    return row, both, qpos, kpos, scale, logs


def attend_tiles(query, both, qpos, kpos, key_scale):
    rows, count, width = query.shape
    parts = both.shape[0]
    row, pair, qspec, kspec, scale, logs = attention_specs(rows, parts, count, width)
    return pl.pallas_call(
        attend_kernel,
        grid=(rows,),
        in_specs=[row, pair, qspec, kspec, scale],
        out_specs=[row, logs],
        out_shape=[
            jax.ShapeDtypeStruct((rows, count, width), jnp.float32),
            jax.ShapeDtypeStruct((rows, count, 2), jnp.float32),
        ],
        name="attend",
    )(query, both, qpos, kpos, key_scale)


def attend_back_tiles(query, both, grad, attended, log_total, qpos, kpos, key_scale):
    rows, count, width = query.shape
    parts = both.shape[0]
    row, pair, qspec, kspec, scale, logs = attention_specs(rows, parts, count, width)
    return pl.pallas_call(
        attend_back_kernel,
        grid=(rows,),
        in_specs=[row, pair, row, row, logs, qspec, kspec, scale],
        out_specs=[row, pair],
        out_shape=[
            jax.ShapeDtypeStruct((rows, count, width), jnp.float32),
            jax.ShapeDtypeStruct(both.shape, jnp.bfloat16),
        ],
        name="attend_back",
    )(query, both, grad, attended, log_total, qpos, kpos, key_scale)


def swap(value, axis, bit):
    size = lax.axis_size(axis)
    return lax.ppermute(value, axis, [(i, i ^ bit) for i in range(size)])


def spread(blocks, axis):
    return lax.all_to_all(blocks, axis, split_axis=0, concat_axis=0, tiled=True)


def others(value):
    return (value, swap(value, "tp", 1), swap(value, "tp", 2), swap(value, "tp", 3))


def in_order(pieces, part):
    odd = part % 2 == 1
    high = part // 2 == 1
    a, b, c, d = pieces
    a, b, c, d = (jnp.where(odd, p, q) for p, q in ((b, a), (a, b), (d, c), (c, d)))
    return tuple(jnp.where(high, p, q) for p, q in ((c, a), (d, b), (a, c), (b, d)))


def reduce_tp(blocks, part):
    total = lax.dynamic_index_in_dim(blocks, part, axis=0, keepdims=False).astype(jnp.float32)
    for bit in range(1, 4):
        block = lax.dynamic_index_in_dim(blocks, part ^ bit, axis=0, keepdims=False)
        total = total + swap(block, "tp", bit).astype(jnp.float32)
    return total


def tie(*values):
    return lax.optimization_barrier(values)


def gather_tp(piece, one, two, first):
    three = swap(one, "tp", 2) if first == 1 else swap(two, "tp", 1)
    return (piece, one, two, three)


def scatter_tp(keep, send, second, axis):
    first = 3 - second
    merged = keep + swap(send.astype(jnp.bfloat16), "tp", first).astype(jnp.float32)
    mine, other = jnp.split(merged, 2, axis=axis)
    return mine + swap(other.astype(jnp.bfloat16), "tp", second).astype(jnp.float32)


def natural_rows(grad, chips):
    width = grad.shape[-1]
    view = grad.reshape(chips, 2, 2, 2, 64, width)
    view = jnp.stack([view[:, 0], view[:, 1, ::-1]], axis=1)
    return view.transpose(1, 3, 0, 2, 4, 5).reshape(2 * 2, -1, width)


def matmul(lhs, rhs, dims):
    return lax.dot_general(lhs, rhs, (dims, ((), ())), preferred_element_type=jnp.float32)


def local_fast(
    tokens,
    cotangent,
    w_query,
    w_key,
    w_value,
    w_out,
    query_gain,
    key_gain,
    attn_gain,
    w_gate,
    w_up,
    w_down,
    mlp_gain,
    group_ids,
    span_order,
):
    low = jnp.bfloat16
    batch_rows, local_len, width = tokens.shape
    members = lax.axis_size("fsdp")
    parts = lax.axis_size("tp")
    chips = members // 2
    member = lax.axis_index("fsdp")
    part = lax.axis_index("tp")
    core = member % 2
    span_len = local_len // 2
    sub = local_len // parts
    count = members * sub
    tile = batch_rows * count
    pair = 2 * HEAD_DIM
    bundle = 4 * 64
    rows_local = w_query.shape[0]
    unit = w_gate.shape[1] // members

    own_tokens = lax.dynamic_slice_in_dim(tokens, part * sub, sub, axis=1)
    own_cotangent = lax.dynamic_slice_in_dim(cotangent, part * sub, sub, axis=1)

    def halves(weight):
        return weight.reshape(rows_local, members, 64)

    packed = jnp.concatenate(
        [halves(w_query), halves(w_key), halves(w_value), jnp.zeros_like(halves(w_value))], axis=2
    ).transpose(1, 0, 2)
    packed = spread(packed, "fsdp").reshape(width, bundle)

    def columns(weight):
        return weight.reshape(rows_local, members, unit).transpose(1, 0, 2)

    packed, gate_up = tie(packed, jnp.stack([columns(w_gate), columns(w_up)], axis=1))
    gate_up = spread(gate_up, "fsdp")
    gate_up, down = tie(gate_up, w_down.reshape(members, unit, rows_local))
    down = spread(down, "fsdp")
    gain_row = jnp.concatenate(
        [query_gain, key_gain, jnp.zeros((bundle - 2 * 64,), query_gain.dtype)]
    )
    packed = jnp.concatenate(
        [packed, jnp.broadcast_to(gain_row[None], (16, bundle)).astype(packed.dtype)], axis=0
    )
    token_low = lax.all_gather(own_tokens.astype(low), "fsdp", axis=1, tiled=True)
    cut = width // 2
    first, second = swap(packed, "tp", 1), swap(packed, "tp", 2)
    third = jnp.concatenate([swap(first[:cut], "tp", 2), swap(second[cut:], "tp", 1)], axis=0)
    near = part // 2 == core
    odd = part % 2 == 1
    mine = [jnp.where(near, packed, second), jnp.where(near, first, third)]
    theirs = [jnp.where(near, second, packed), jnp.where(near, third, first)]
    own_half = [jnp.where(odd, mine[1], mine[0]), jnp.where(odd, mine[0], mine[1])]
    other_half = swap(
        jnp.stack([jnp.where(odd, theirs[1], theirs[0]), jnp.where(odd, theirs[0], theirs[1])]),
        "fsdp",
        1,
    )

    norm_gains = jnp.concatenate(
        [attn_gain[None], mlp_gain[None], jnp.zeros((14, attn_gain.shape[0]), attn_gain.dtype)]
    )
    out_rows = lax.all_gather(
        jnp.concatenate([w_out, norm_gains.astype(w_out.dtype)], axis=0),
        "fsdp",
        axis=1,
        tiled=True,
    )
    gain_attn = out_rows[w_out.shape[0]].astype(jnp.float32)
    gain_mlp = out_rows[w_out.shape[0] + 1].astype(jnp.float32)
    out_full = lax.all_gather(
        out_rows[: w_out.shape[0]].reshape(2 * chips, 64, width), "tp", axis=1, tiled=True
    ).reshape(width, width)

    index = jnp.arange(members, dtype=jnp.int32)[:, None] * local_len
    index = (index + jnp.arange(sub, dtype=jnp.int32)[None, :]).reshape(count)
    index = index[None, :] + (part ^ jnp.arange(parts, dtype=jnp.int32))[:, None] * sub
    spans = jnp.arange(span_order.shape[0], dtype=jnp.int32)
    picked = jnp.sum(
        jnp.where((index // span_len)[..., None] == spans, span_order, 0), axis=-1
    )
    all_pos = picked * span_len + index % span_len
    query_pos = all_pos[0]
    inv_freq = jnp.power(
        rope_base, -(jnp.arange(64, dtype=jnp.float32) * 2.0 / HEAD_DIM)
    )
    angles = query_pos.astype(jnp.float32)[:, None] * jnp.tile(inv_freq, 2)[None, :]
    cosine = jnp.cos(angles)[None]
    sine = (jnp.where(core == 0, 1.0, -1.0) * jnp.sin(angles))[None]

    def rotate(value, direction):
        own, other = value[..., :HEAD_DIM], value[..., HEAD_DIM:]
        turned = direction * sine
        return jnp.concatenate(
            [own * cosine - other * turned, other * cosine + own * turned], axis=-1
        )

    weight_pieces = [own_half[0], own_half[1], other_half[0], other_half[1]]
    acts = [
        matmul(token_low, piece[:width], ((2,), (0,))) for piece in weight_pieces
    ]

    def lanes(pieces, at):
        return jnp.concatenate([piece[..., at * 64 : at * 64 + 64] for piece in pieces], axis=-1)

    queries, keys, values = (lanes(acts, at) for at in range(3))
    gain_rows = [piece[width].astype(jnp.float32) for piece in weight_pieces]
    gain_query, gain_key = lanes(gain_rows, 0), lanes(gain_rows, 1)
    key_low = rotate(keys * gain_key, 1.0).astype(low)
    both = jnp.concatenate([key_low, values.astype(low)], axis=-1)
    both, gate_up = tie(both, gate_up)
    both = jnp.stack(others(both))
    gate_own, up_own = gate_up[:, 0].reshape(width, unit), gate_up[:, 1].reshape(width, unit)
    near_weights = [swap(weight, "tp", bit) for weight in (gate_own, up_own) for bit in (1, 2)]
    square_sums = lax.psum(
        jnp.stack([jnp.sum(queries * queries, axis=-1), jnp.sum(keys * keys, axis=-1)]), "fsdp"
    )
    scales = lax.rsqrt(square_sums / width + epsilon)
    query_scale, key_scale = scales[0][..., None], scales[1][..., None]
    all_key_scale = jnp.stack(others(scales[1])).reshape(parts, batch_rows, 1, count)
    query_low = rotate(queries * query_scale * gain_query, 1.0).astype(low)
    qpos = query_pos[:, None]
    kpos = all_pos[:, None, :]
    query_low, down = tie(query_low, down)
    down_own = down.transpose(1, 0, 2).reshape(unit, width)
    near_weights += [swap(down_own, "tp", bit) for bit in (1, 2)]
    attended, log_total = attend_tiles(query_low, both, qpos, kpos, all_key_scale)

    places = [(chip, half, side) for chip in range(chips) for half in range(2) for side in range(2)]

    def to_tokens(value):
        blocks = value.reshape(batch_rows, members, sub, pair).transpose(1, 0, 2, 3)
        blocks = spread(blocks, "fsdp")
        return jnp.concatenate(
            [
                blocks[2 * chip + side][..., (half ^ side) * HEAD_DIM :][..., :HEAD_DIM]
                for chip, half, side in places
            ],
            axis=-1,
        )

    def to_heads(value):
        def lanes_at(chip, half, side):
            at = places.index((chip, half, side)) * HEAD_DIM
            return value[..., at : at + HEAD_DIM]

        blocks = jnp.stack(
            [
                jnp.concatenate(
                    [lanes_at(chip, side, side), lanes_at(chip, 1 - side, side)], axis=-1
                )
                for chip in range(chips)
                for side in range(2)
            ]
        )
        return spread(blocks, "fsdp").transpose(1, 0, 2, 3).reshape(batch_rows, count, pair)

    attended_low = attended.astype(low)
    attended_low, *near_weights = tie(attended_low, *near_weights)
    gate_all = jnp.concatenate(gather_tp(gate_own, *near_weights[:2], 1), axis=1)
    up_all = jnp.concatenate(gather_tp(up_own, *near_weights[2:4], 2), axis=1)
    down_all = jnp.concatenate(gather_tp(down_own, *near_weights[4:], 1), axis=0)
    branch_attn = matmul(to_tokens(attended_low), out_full, ((2,), (0,)))
    attn_norm = lax.rsqrt(jnp.mean(branch_attn * branch_attn, axis=-1, keepdims=True) + epsilon)
    hidden = own_tokens + branch_attn * attn_norm * gain_attn
    hidden_low = lax.all_gather(hidden.astype(low), "fsdp", axis=1, tiled=True)

    gate_act = matmul(hidden_low, gate_all, ((2,), (0,)))
    up_act = matmul(hidden_low, up_all, ((2,), (0,)))
    gate_sigma = jax.nn.sigmoid(gate_act)
    mixed_low = (gate_act * gate_sigma * up_act).astype(low)
    attended_all = lax.all_gather(attended_low, "fsdp", axis=2, tiled=True)
    branch_low, attended_all = tie(
        matmul(mixed_low, down_all, ((2,), (0,))).astype(low), attended_all
    )
    branch_mlp = lax.psum_scatter(
        branch_low,
        "fsdp",
        scatter_dimension=1,
        tiled=True,
    ).astype(jnp.float32)
    mlp_norm = lax.rsqrt(jnp.mean(branch_mlp * branch_mlp, axis=-1, keepdims=True) + epsilon)
    layer_own = hidden + branch_mlp * mlp_norm * gain_mlp

    def whole_span(pieces):
        pieces = in_order(pieces, part)
        return jnp.concatenate(pieces, axis=1).astype(jnp.float32)

    grad_gain_mlp, grad_branch_mlp = norm_back(branch_mlp, mlp_norm, gain_mlp, own_cotangent)
    grad_mlp_low = lax.all_gather(grad_branch_mlp.astype(low), "fsdp", axis=1, tiled=True)
    layer_pieces = others(layer_own.astype(low))
    grad_mixed = matmul(grad_mlp_low, down_all, ((2,), (1,)))
    grad_gate_act = (
        grad_mixed * up_act * gate_sigma * (1.0 + gate_act * (1.0 - gate_sigma))
    ).astype(low)
    grad_up_act = (grad_mixed * gate_act * gate_sigma).astype(low)
    mlp_back_in = matmul(grad_gate_act, gate_all, ((2,), (1,))) + matmul(
        grad_up_act, up_all, ((2,), (1,))
    )
    mlp_back_low, *layer_pieces = tie(mlp_back_in.astype(low), *layer_pieces)
    layer_out = whole_span(layer_pieces)
    grad_hidden = own_cotangent + lax.psum_scatter(
        mlp_back_low, "fsdp", scatter_dimension=1, tiled=True
    ).astype(jnp.float32)

    hidden_flat = hidden_low.reshape(tile, width)
    grad_flat = grad_mlp_low.reshape(tile, width)

    def block_pair(value, a, b):
        flat = value.reshape(tile, -1)
        return jnp.concatenate(
            [flat[:, a * unit : (a + 1) * unit], flat[:, b * unit : (b + 1) * unit]], axis=1
        )

    grad_down_w = scatter_tp(
        matmul(block_pair(mixed_low, 0, 2), grad_flat, ((0,), (0,))),
        matmul(block_pair(mixed_low, 1, 3), grad_flat, ((0,), (0,))),
        2,
        0,
    )
    grad_gate_w = scatter_tp(
        matmul(hidden_flat, block_pair(grad_gate_act, 0, 1), ((0,), (0,))),
        matmul(hidden_flat, block_pair(grad_gate_act, 2, 3), ((0,), (0,))),
        1,
        1,
    )
    grad_up_w = scatter_tp(
        matmul(hidden_flat, block_pair(grad_up_act, 0, 2), ((0,), (0,))),
        matmul(hidden_flat, block_pair(grad_up_act, 1, 3), ((0,), (0,))),
        2,
        1,
    )
    down_back = spread(
        grad_down_w.astype(low).reshape(unit, members, rows_local).transpose(1, 0, 2), "fsdp"
    )

    def unit_back(value):
        return spread(value.astype(low).reshape(members, rows_local, unit), "fsdp")

    def unit_columns(blocks):
        return blocks.transpose(1, 0, 2).reshape(rows_local, members * unit).astype(jnp.float32)

    gate_back = unit_back(grad_gate_w)
    up_back = unit_back(grad_up_w)

    grad_gain_attn, grad_branch_attn = norm_back(branch_attn, attn_norm, gain_attn, grad_hidden)
    grad_attn_low = grad_branch_attn.astype(low)
    grad_attended = to_heads(matmul(grad_attn_low, out_full, ((2,), (1,))).astype(low))
    feature_blocks = jnp.concatenate(
        [
            grad_attn_low.reshape(batch_rows * sub, width),
            grad_gain_attn[None].astype(low),
            grad_gain_mlp[None].astype(low),
            jnp.zeros((14, width), low),
        ],
        axis=0,
    )
    feature_blocks = spread(
        feature_blocks.reshape(-1, members, rows_local).transpose(1, 0, 2), "fsdp"
    )
    own_features = feature_blocks[:, : batch_rows * sub].reshape(
        members, batch_rows, sub, rows_local
    )
    gain_sums = jnp.sum(
        feature_blocks[:, batch_rows * sub :].astype(jnp.float32), axis=0
    )
    own_features = own_features.transpose(1, 0, 2, 3).reshape(batch_rows, count, rows_local)
    in_group = (group_ids[:, 0][:, None] == jnp.arange(GROUPS, dtype=jnp.int32)[None, :]).astype(
        low
    )
    out_blocks = []
    for group in range(GROUPS):
        masked = own_features * in_group[:, group][:, None, None]
        product = matmul(
            attended_all.reshape(tile, -1), masked.reshape(tile, rows_local), ((0,), (0,))
        )
        out_blocks.append(natural_rows(product.astype(low), chips))
    out_blocks.append(
        jnp.broadcast_to(gain_sums.astype(low)[None], (parts,) + gain_sums.shape)
    )
    out_sum = reduce_tp(jnp.concatenate(out_blocks, axis=1), part)
    block_rows = w_out.shape[0]
    grad_out_groups = out_sum[: GROUPS * block_rows].reshape(GROUPS, block_rows, rows_local)
    grad_out = jnp.sum(grad_out_groups, axis=0)
    grad_attn_gain = out_sum[GROUPS * block_rows]
    grad_mlp_gain = out_sum[GROUPS * block_rows + 1]

    grad_query_rot, grad_both = attend_back_tiles(
        query_low, both, grad_attended, attended, log_total, qpos, kpos, all_key_scale
    )
    grad_both = sum(
        value.astype(jnp.float32)
        for value in [grad_both[0]] + [swap(grad_both[bit], "tp", bit) for bit in range(1, 4)]
    )
    grad_qn = rotate(grad_query_rot, -1.0)
    grad_kn = rotate(grad_both[..., :pair], -1.0)
    gained_query = grad_qn * gain_query
    gained_key = grad_kn * gain_key
    cross_sums = lax.psum(
        jnp.stack(
            [jnp.sum(queries * gained_query, axis=-1), jnp.sum(keys * gained_key, axis=-1)]
        ),
        "fsdp",
    )
    grad_gain_query = jnp.sum(grad_qn * queries * query_scale, axis=(0, 1))
    grad_gain_key = jnp.sum(grad_kn * keys, axis=(0, 1))
    grad_queries = (
        query_scale * gained_query - queries * query_scale**3 * cross_sums[0][..., None] / width
    ).astype(low)
    grad_keys = (
        gained_key - keys * key_scale**2 * cross_sums[1][..., None] / width
    ).astype(low)
    grad_values = grad_both[..., pair:].astype(low)
    grad_acts = [
        jnp.concatenate(
            [
                value[..., at * 64 : at * 64 + 64]
                for value in (grad_queries, grad_keys, grad_values, jnp.zeros_like(grad_values))
            ],
            axis=-1,
        )
        for at in range(4)
    ]
    attn_back_in = sum(
        matmul(grad, piece[:width], ((2,), (1,))) for grad, piece in zip(grad_acts, weight_pieces)
    )
    attn_back_low, down_back = tie(attn_back_in.astype(low), down_back)
    grad_down = down_back.reshape(members * unit, rows_local).astype(jnp.float32)
    input_own = grad_hidden + lax.psum_scatter(
        attn_back_low, "fsdp", scatter_dimension=1, tiled=True
    ).astype(jnp.float32)
    input_grad = whole_span(others(input_own.astype(low)))

    token_flat = token_low.reshape(tile, width)

    def with_gain(at):
        product = matmul(token_flat, grad_acts[at].reshape(tile, bundle), ((0,), (0,)))
        gains = jnp.concatenate(
            [
                grad_gain_query[at * 64 : at * 64 + 64],
                grad_gain_key[at * 64 : at * 64 + 64],
                jnp.zeros((bundle - 2 * 64,), jnp.float32),
            ]
        )
        return jnp.concatenate(
            [product.astype(low), jnp.broadcast_to(gains[None], (16, bundle)).astype(low)], axis=0
        )

    sent = swap(jnp.stack([with_gain(2), with_gain(3)]), "fsdp", 1)
    kept = jnp.stack([with_gain(0), with_gain(1)])
    proj_blocks = jnp.where(
        core == 0, jnp.concatenate([kept, sent]), jnp.concatenate([sent, kept])
    )
    proj_sum = reduce_tp(proj_blocks, part)
    grad_query_gain = proj_sum[width, :64]
    grad_key_gain = proj_sum[width, 64:128]
    proj_low, gate_back, up_back = tie(proj_sum[:width].astype(low), gate_back, up_back)
    grad_gate = unit_columns(gate_back)
    grad_up = unit_columns(up_back)
    proj_back = spread(proj_low.reshape(members, rows_local, bundle), "fsdp")

    def natural_columns(at):
        block = proj_back[:, :, at * 64 : at * 64 + 64].astype(jnp.float32)
        return block.transpose(1, 0, 2).reshape(rows_local, members * 64)

    return (
        layer_out,
        input_grad,
        natural_columns(0),
        natural_columns(1),
        natural_columns(2),
        grad_out,
        grad_query_gain,
        grad_key_gain,
        grad_attn_gain,
        grad_gate,
        grad_up,
        grad_down,
        grad_mlp_gain,
        grad_out_groups,
    )


def solution(mesh):
    in_specs = (
        P(None, "fsdp", None),
        P(None, "fsdp", None),
        P("fsdp", "tp"),
        P("fsdp", "tp"),
        P("fsdp", "tp"),
        P("tp", "fsdp"),
        P(("tp", "fsdp")),
        P(("tp", "fsdp")),
        P("fsdp"),
        P("fsdp", "tp"),
        P("fsdp", "tp"),
        P("tp", "fsdp"),
        P("fsdp"),
        P(),
        P(),
    )
    out_specs = (
        P(None, "fsdp", None),
        P(None, "fsdp", None),
        P("fsdp", "tp"),
        P("fsdp", "tp"),
        P("fsdp", "tp"),
        P("tp", "fsdp"),
        P(("tp", "fsdp")),
        P(("tp", "fsdp")),
        P("fsdp"),
        P("fsdp", "tp"),
        P("fsdp", "tp"),
        P("tp", "fsdp"),
        P("fsdp"),
        P(None, "tp", "fsdp"),
    )
    heads = 2048 // HEAD_DIM
    members, parts = mesh.shape["fsdp"], mesh.shape["tp"]
    fits = parts == 4 and heads // parts * 2 == members
    body = local_fast if fits else local
    return jax.shard_map(body, mesh=mesh, in_specs=in_specs, out_specs=out_specs, check_vma=False)
```
